256 devices in a mesh: space: 32 (over z_lo, y, core), dom: 8 (over z_hi, x).
Axes of the slice: x: 4, y: 4, z: 8 (z_hi: 2, z_lo: 4; z = z_hi * 4 + z_lo), core: 2. Of those that a mesh axis runs over, the one named last changes fastest.
Arguments:
- water_depth: float32 [16, 32, 256, 512], P('dom', 'space'), may hold values from 0 to 1.5
- infiltrated: float32 [16, 32, 256, 512], P('dom', 'space'), may hold values from 0.2 to 2
- terrain: float32 [32, 256, 512], P('space'), may hold values from -3 to 3
- land_mask: int32 [32, 256, 512], P('space'), may hold values from 0 to 1
- forcing: bfloat16 [2, 2, 32, 256, 512], P(None, None, 'space', 'dom'), may hold values from 0.049804688 to 1.5
- observed: bfloat16 [2, 32, 256, 512], P(None, 'space'), may hold values from 0 to 3.6
- conductivity: float32 [16], replicated, may hold values from 0.05 to 0.6
- suction: float32 [16], replicated, may hold values from 0.1 to 2
- manning: float32 [16], replicated, may hold values from 0.5 to 2
- assignment: int32 [16], P('dom'), may hold values from 0 to 15, each once
- ancestors: int32 [16], P('dom'), may hold values from 0 to 15, as said below
- prior_weight: float32 [16], P('dom'), may hold values from 0.01 to 1
Outputs:
- final_depth: float32 [16, 32, 256, 512], P('dom', 'space')
- final_infiltrated: float32 [16, 32, 256, 512], P('dom', 'space')
- weights: float32 [16], P('dom')
The draws below stay inside these ranges and needn't reach their ends.
Inputs may be any that keep to these rules, and one draw needn't show every extreme that they name: `ancestors`: the ancestor of slot s is a slot of its own group, 2 * (s // 2) to 2 * (s // 2) + 1; slot 0's ancestor is 0 and the last slot's is itself.
All inputs are finite; a program needn't handle non-finite values.
Results may differ from the reference program's by a relative error of at most 0.0003.
Values may be sent and summed in bfloat16 or wider, within the bound.
No kernel may reach another device: no remote copies, remote signals or barrier semaphores. Data moves between devices by JAX's collectives and lax.ppermute only.
A program may use at most 64 MiB of HBM per device.

```python
import math
import jax
import jax.numpy as jnp
from jax import lax

CY = 256
CX = 512
P_DEV = 2
TX = 4
SUB = 6
HOURS = 2
PARTS_SIZE = 16
TILES = 32
TY = 8
N_DOM = 8


def draw_land_mask(key, part):
    tiles = jnp.arange(TILES, dtype=jnp.int32)[:, None, None]
    limit = 300 + 600 * tiles // max(TILES - 1, 1)
    roll = jax.random.randint(key, (TILES, CY, CX), 0, 1000)
    return (roll < limit).astype(jnp.int32)


def draw_observed(key, part):
    shape = (HOURS, TILES, CY, CX)
    tiles = jnp.arange(TILES, dtype=jnp.float32)[None, :, None, None]
    scale = 1.0 + 2.0 * tiles / max(TILES - 1, 1)
    base = jax.random.uniform(key, shape, jnp.float32, 0.0, 1.2)
    return (base * scale).astype(jnp.bfloat16)


def draw_ancestors(key, part):
    offsets = jax.random.randint(key, (PARTS_SIZE,), 0, P_DEV)
    offsets = offsets.at[0].set(0).at[PARTS_SIZE - 1].set(P_DEV - 1)
    slots = jnp.arange(PARTS_SIZE, dtype=jnp.int32)
    return slots // P_DEV * P_DEV + offsets


def levels(key, shape, split, low, high):
    level, own = 1.0, jax.random.fold_in(key, 6)
    for axis_at, blocks in split:
        steps = jnp.exp(jax.random.uniform(jax.random.fold_in(own, axis_at), (blocks,), jnp.float32, low / len(split), high / len(split)))
        level = level * jnp.repeat(steps, shape[axis_at] // blocks).reshape([-1 if axis == axis_at else 1 for axis in range(len(shape))])
    return level


def centred(rng, extent, deviation, bound, pieces=(), kind=jnp.bfloat16):
    drawn = deviation * jax.random.normal(rng, extent, jnp.float32)
    if pieces:
        drawn = drawn * levels(rng, extent, pieces, -0.22, 0.18)
    return jnp.clip(drawn, -bound, bound).astype(kind)


def setup_inputs(seed: int = 0) -> dict:
    key_list = jax.random.split(jax.random.key(seed), 13)
    return {
        "water_depth": jnp.clip(1.5 * jax.random.uniform(key_list[0], (PARTS_SIZE, TILES, CY, CX), jnp.float32) ** levels(key_list[0], (PARTS_SIZE, TILES, CY, CX), ((0, 8), (1, 32)), -0.2, 0.2), 0.0, 1.5),
        "infiltrated": jnp.clip(0.2 + 1.8 * jax.random.uniform(key_list[1], (PARTS_SIZE, TILES, CY, CX), jnp.float32) ** levels(key_list[1], (PARTS_SIZE, TILES, CY, CX), ((0, 8), (1, 32)), -0.2, 0.2), 0.2, 2.0),
        "terrain": centred(key_list[2], (TILES, CY, CX), 0.5, 3.0, ((0, 32),), jnp.float32),
        "land_mask": draw_land_mask(jax.random.fold_in(key_list[12], 71), 0),
        "forcing": jnp.clip(jnp.exp(math.log(1.5) - 3.4051113 * jax.random.uniform(key_list[4], (HOURS, 2, TILES, CY, CX), jnp.float32) ** levels(key_list[4], (HOURS, 2, TILES, CY, CX), ((2, 32), (3, 8)), -0.2, 0.2)), 0.049804688, 1.5).astype(jnp.bfloat16),
        "observed": draw_observed(jax.random.fold_in(key_list[12], 71), 0),
        "conductivity": jnp.clip(jnp.exp(jax.random.uniform(key_list[6], (PARTS_SIZE,), jnp.float32, math.log(0.05), math.log(0.6))), 0.05, 0.6),
        "suction": jnp.clip(jnp.exp(jax.random.uniform(key_list[7], (PARTS_SIZE,), jnp.float32, math.log(0.1), math.log(2.0))), 0.1, 2.0),
        "manning": jnp.clip(jnp.exp(jax.random.uniform(key_list[8], (PARTS_SIZE,), jnp.float32, math.log(0.5), math.log(2.0))), 0.5, 2.0),
        "assignment": jax.random.permutation(key_list[9], PARTS_SIZE).astype(jnp.int32),
        "ancestors": draw_ancestors(jax.random.fold_in(key_list[12], 71), 0),
        "prior_weight": jnp.clip(jnp.exp(math.log(1.0) - 4.6051702 * jax.random.uniform(key_list[11], (PARTS_SIZE,), jnp.float32) ** levels(key_list[11], (PARTS_SIZE,), ((0, 8),), -0.2, 0.2)), 0.01, 1.0),
    }


time_step = 0.01
slope_floor = 0.1
sharpness = 20.0

def to_grid(tiles):
    lead = tiles.shape[:-3]
    count = len(lead)
    blocks = tiles.reshape(lead + (TY, TX, CY, CX))
    blocks = jnp.swapaxes(blocks, count + 1, count + 2)
    return blocks.reshape(lead + (TY * CY, TX * CX))

def to_tiles(grid):
    lead = grid.shape[:-2]
    count = len(lead)
    blocks = grid.reshape(lead + (TY, CY, TX, CX))
    blocks = jnp.swapaxes(blocks, count + 1, count + 2)
    return blocks.reshape(lead + (TY * TX, CY, CX))

def pad_field(field):
    tall = jnp.pad(field, ((1, 1), (0, 0)))
    return jnp.pad(tall, ((0, 0), (1, 1)), mode='wrap')

def face_flux(depth_a, depth_b, level_a, level_b, rough):
    slope = level_b - level_a
    mean_depth = 0.5 * (depth_a + depth_b)
    return -jnp.power(mean_depth, 5.0 / 3.0) * slope / (rough * jnp.sqrt(jnp.abs(slope) + slope_floor))

def substep(water, soaked, ground, net_rain, land, conduct, suction_p, rough):
    padded = pad_field(water)
    level = padded + ground
    flux_cols = face_flux(padded[1:-1, :-1], padded[1:-1, 1:], level[1:-1, :-1], level[1:-1, 1:], rough)
    flux_rows = face_flux(padded[:-1, 1:-1], padded[1:, 1:-1], level[:-1, 1:-1], level[1:, 1:-1], rough)
    outflow = flux_cols[:, 1:] - flux_cols[:, :-1] + flux_rows[1:, :] - flux_rows[:-1, :]
    ponded = jnp.maximum(water - time_step * outflow + time_step * net_rain, 0.0)
    capacity = conduct * (1.0 + suction_p / soaked)
    intake = jnp.minimum(time_step * capacity, ponded)
    return ((ponded - intake) * land, soaked + intake * land)

def reference(water_depth, infiltrated, terrain, land_mask, forcing, observed, conductivity, suction, manning, assignment, ancestors, prior_weight):
    owners = assignment[ancestors]
    group_mean = jnp.repeat(lax.optimization_barrier(jnp.mean(prior_weight.reshape(N_DOM, P_DEV), axis=1)), P_DEV)
    land = to_grid(land_mask).astype(jnp.float32)
    ground = pad_field(to_grid(terrain))
    rains = [to_grid(forcing[hour, 0].astype(jnp.float32) - forcing[hour, 1].astype(jnp.float32)) for hour in range(HOURS)]
    seen = [to_grid(observed[hour].astype(jnp.float32)) for hour in range(HOURS)]

    def particle(items):
        water_tiles, soak_tiles, conduct, suction_p, rough = items
        water = to_grid(water_tiles)
        soaked = to_grid(soak_tiles)
        misfit = jnp.zeros((), jnp.float32)
        for hour in range(HOURS):
            net_rain = rains[hour]

            def advance(index, carry):
                return substep(carry[0], carry[1], ground, net_rain, land, conduct, suction_p, rough)
            water, soaked = lax.fori_loop(0, SUB, advance, (water, soaked))
            gap = water - seen[hour]
            square = gap * gap
            misfit = misfit + jnp.sum(land * square / (1.0 + square))
        return (to_tiles(water), to_tiles(soaked), misfit)
    final_depth, final_soak, misfit = lax.map(particle, (water_depth[ancestors], infiltrated[ancestors], conductivity[owners], suction[owners], manning[owners]))
    cells = HOURS * jnp.sum(land)
    raw = group_mean * jnp.exp(-sharpness * misfit / cells)
    weights = raw / jnp.sum(raw)
    return (final_depth, final_soak, weights)
```

```python
import jax
import jax.numpy as jnp
from jax import lax
from jax.experimental import pallas as pl
from jax.experimental.pallas import tpu as pltpu
from jax.sharding import PartitionSpec as P

TX = 4
SUB = 6
HOURS = 2
TIME_STEP = 0.01
SLOPE_FLOOR = 0.1
SHARPNESS = 20.0

CY, CX = 256, 512
HALO = SUB * HOURS
COLS = 16
EXT = CY + 2 * HALO
STRIP = EXT // 8
LANES = 128
CHUNKS = CX // LANES
ROWS = 5
WIDE = 2 * CHUNKS + 1

RAIN_SCALE = 4096.0
WATER_SCALE = 20000.0
SOAK_SCALE = 16000.0
GROUND_SCALE = 10000.0

FIELDS = 8
SCALES = (WATER_SCALE, WATER_SCALE, SOAK_SCALE, SOAK_SCALE, GROUND_SCALE, 1.0, RAIN_SCALE, RAIN_SCALE)
FROM_EAST = (4, 0, 5, 1, 2, 6, 3, 7)
FROM_WEST = (3, 7, 2, 6, 1, 5, 0, 4)


def lane_ids(rows):
    return lax.broadcasted_iota(jnp.int32, (rows, LANES), 1)


def coded(value, scale):
    scaled = value * scale
    return (scaled + jnp.where(scaled >= 0, 0.5, -0.5)).astype(jnp.int32)


def rolled(value, shift, axis=1):
    shift = shift % value.shape[axis]
    return value if shift == 0 else pltpu.roll(value, shift, axis)


def pack_kernel(anc, water, soak, terrain, land, rain, west_out, east_out, north_out, south_out, rows_n, rows_s):
    slots = [anc[p] % 2 for p in range(2)]

    def part(field, rows, lanes):
        if field < 2:
            return water[slots[field], 0, rows, lanes]
        if field < 4:
            return soak[slots[field - 2], 0, rows, lanes]
        if field == 4:
            return terrain[0, rows, lanes]
        return land[0, rows, lanes].astype(jnp.float32)

    first = pl.ds(0, LANES)
    last = pl.ds(CX - LANES, LANES)

    def edges(d, carry):
        rows = pl.ds(pl.multiple_of(d * 32, 32), 32)
        group = lane_ids(32) // COLS
        to_west = jnp.zeros((32, LANES), jnp.int32)
        to_east = jnp.zeros((32, LANES), jnp.int32)
        for f in range(FIELDS):
            if f < 6:
                a = coded(part(f, rows, first), SCALES[f])
                b = coded(part(f, rows, last), SCALES[f])
            else:
                a = rain[d, f - 6, :, first].astype(jnp.int32)
                b = rain[d, f - 6, :, last].astype(jnp.int32)
            at = FROM_EAST[f]
            to_west = jnp.where(group == at, rolled(a, at * COLS), to_west)
            at = FROM_WEST[f]
            to_east = jnp.where(group == at, rolled(b, (at + 1) * COLS - LANES), to_east)
        west_out[rows, :] = to_west.astype(jnp.int16)
        east_out[rows, :] = to_east.astype(jnp.int16)
        return carry

    lax.fori_loop(0, CY // 32, edges, 0)

    for f in range(FIELDS):
        put = pl.ds(HALO * f, HALO)
        for c in range(CHUNKS):
            lanes = pl.ds(c * LANES, LANES)
            if f < 6:
                a = coded(part(f, pl.ds(0, 16), lanes), SCALES[f])
                b = coded(part(f, pl.ds(CY - 16, 16), lanes), SCALES[f])
            else:
                a = rain[0, f - 6, pl.ds(0, 16), lanes].astype(jnp.int32)
                b = rain[7, f - 6, pl.ds(16, 16), lanes].astype(jnp.int32)
            rows_n[c, put, :] = a[:HALO]
            rows_s[c, put, :] = b[16 - HALO:]
    for c in range(CHUNKS):
        lanes = pl.ds(c * LANES, LANES)
        north_out[:, lanes] = rows_n[c].astype(jnp.int16)
        south_out[:, lanes] = rows_s[c].astype(jnp.int16)


def step_kernel(anc, owner, cond, suction, manning, water, soak, terrain, land, rain, seen,
                east_in, west_in, north_in, south_in, corner_n, corner_s,
                depth_out, soak_out, misfit_out,
                nat, east, west, rows_ns, W, S, dgc, dgr, L, own, R, O, coef, acc):
    f32 = jnp.float32
    slots = [anc[p] % 2 for p in range(2)]
    lane8 = lane_ids(8)
    lane_e = lane_ids(EXT)
    body = pl.ds(HALO, CY)
    top = pl.ds(0, HALO)
    bottom = pl.ds(HALO + CY, HALO)

    for ref, got, col in ((east, east_in, 0), (west, west_in, 1)):
        lanes = pl.ds(col * LANES, LANES)
        ref[body, :] = got[:, :].astype(jnp.int32)
        ref[top, :] = corner_n[:, lanes].astype(jnp.int32)[16 - HALO:]
        ref[bottom, :] = corner_s[:, lanes].astype(jnp.int32)[:HALO]
    for c in range(CHUNKS):
        lanes = pl.ds(c * LANES, LANES)
        rows_ns[0, c] = north_in[:, lanes].astype(jnp.int32)
        rows_ns[1, c] = south_in[:, lanes].astype(jnp.int32)

    def decode(value, f):
        return value.astype(f32) * (1.0 / SCALES[f])

    def tile_rows(f):
        for c in range(CHUNKS):
            lanes = pl.ds(c * LANES, LANES)
            if f < 2:
                nat[c, body, :] = water[slots[f], 0, :, lanes]
            elif f < 4:
                nat[c, body, :] = soak[slots[f - 2], 0, :, lanes]
            elif f == 4:
                nat[c, body, :] = terrain[0, :, lanes]
            elif f == 5:
                nat[c, body, :] = land[0, :, lanes].astype(f32)
            else:
                for d in range(8):
                    nat[c, pl.ds(HALO + 32 * d, 32), :] = decode(rain[d, f - 6, :, lanes].astype(jnp.int32), f)
            put = pl.ds(HALO * f, HALO)
            nat[c, top, :] = decode(rows_ns[0, c, put, :], f)
            nat[c, bottom, :] = decode(rows_ns[1, c, put, :], f)

    def column_halo(f0, f1, fill):
        group = lane_e // COLS
        x = jnp.full((EXT, LANES), fill, f32)
        for f, ref, table, at in ((f1, east, FROM_EAST, 0), (f0, west, FROM_WEST, 3), (f0, east, FROM_EAST, 4), (f1, west, FROM_WEST, 7)):
            x = jnp.where(group == at, decode(rolled(ref[...], (at - table[f]) * COLS), f), x)
        nat[CHUNKS] = x

    def strip(c, j):
        return nat[c, pl.ds(j, 8, stride=STRIP), :]

    def shifted_strips(j):
        parts = [rolled(strip(c, j), 64) for c in range(CHUNKS + 1)]
        low = lane8 < 64
        return [jnp.where(low, parts[k - 1], parts[k]) for k in range(CHUNKS + 1)]

    def put_strips(dest, first, second, fix=lambda v: v):
        def one(j, carry):
            if first:
                for c in range(CHUNKS):
                    dest[j, c] = fix(strip(c, j))
            if second:
                for k, v in enumerate(shifted_strips(j)):
                    dest[j, CHUNKS + k] = fix(v)
            return carry

        lax.fori_loop(0, STRIP, one, 0)

    column_halo(0, 1, 0.0)
    tile_rows(0)
    put_strips(W, True, False)
    tile_rows(1)
    put_strips(W, False, True)
    column_halo(2, 3, 1.0)
    guard = lambda v: jnp.maximum(v, 0.1)
    tile_rows(2)
    put_strips(S, True, False, guard)
    tile_rows(3)
    put_strips(S, False, True, guard)
    column_halo(5, 5, 0.0)
    tile_rows(5)
    put_strips(L, True, True)
    for h in range(HOURS):
        column_halo(6 + h, 6 + h, 0.0)
        tile_rows(6 + h)
        put_strips(R.at[h], True, True, lambda v: v * TIME_STEP)
    for h in range(HOURS):
        for c in range(CHUNKS):
            nat[c, body, :] = seen[h, 0, :, pl.ds(c * LANES, LANES)].astype(f32)
        put_strips(O.at[h], True, True)
    column_halo(4, 4, 0.0)
    tile_rows(4)
    put_strips(own, True, True)
    last_lane = lane8 == LANES - 1
    first_lane = lane8 == 0

    def ground_steps(j, carry):
        g = [own[j, c] for c in range(WIDE)]
        r = [rolled(v, -1) for v in g]
        below = jnp.where(j == STRIP - 1, 0, j + 1)
        for c in range(WIDE):
            dgc[j, c] = jnp.where(last_lane, r[(c + 1) % WIDE], r[c]) - g[c]
            n = own[below, c]
            n = jnp.where(j == STRIP - 1, rolled(n, -1, 0), n)
            dgr[j, c] = n - g[c]
        return carry

    lax.fori_loop(0, STRIP, ground_steps, 0)

    row_of = lax.broadcasted_iota(jnp.int32, (8, LANES), 0) * STRIP

    def own_cells(j, carry):
        row = row_of + j
        inside = (row >= HALO) & (row < HALO + CY)
        for c in range(WIDE):
            keep = inside
            if c == CHUNKS:
                keep = inside & (lane8 >= 64)
            if c == WIDE - 1:
                keep = inside & (lane8 < 64)
            own[j, c] = jnp.where(keep, L[j, c], 0.0)
        return carry

    lax.fori_loop(0, STRIP, own_cells, 0)

    for k in range(3):
        pair = []
        for p in range(2):
            o = owner[slots[p]]
            if k == 0:
                pair.append(jnp.full((8, LANES), TIME_STEP * 0.5 ** (5.0 / 3.0), f32) / jnp.full((8, LANES), manning[o], f32))
            elif k == 1:
                pair.append(jnp.full((8, LANES), TIME_STEP * cond[o], f32))
            else:
                pair.append(jnp.full((8, LANES), TIME_STEP * cond[o] * suction[o], f32))
        for c in range(WIDE):
            v = pair[0] if c < CHUNKS else pair[1]
            if c == CHUNKS:
                v = jnp.where(lane8 < 32, pair[0], pair[1])
            if c == WIDE - 1:
                v = jnp.where(lane8 < 96, pair[1], pair[0])
            coef[k, c] = v

    def face(a, b, dg):
        total = a + b
        slope = (b - a) + dg
        return jnp.exp2(lax.log2(total) * (5.0 / 3.0)) * slope * lax.rsqrt(jnp.abs(slope) + SLOPE_FLOOR)

    def substep(h):
        for c in range(WIDE):
            W[STRIP, c] = rolled(W[0, c], -1, 0)
        start = tuple(
            rolled(face(W[STRIP - 1, c], W[STRIP, c], dgr[STRIP - 1, c]), 1, 0) for c in range(WIDE)
        )

        def block(i, edge):
            edge = list(edge)
            w = [W[i * ROWS, c] for c in range(WIDE)]
            for u in range(ROWS):
                j = i * ROWS + u
                r = [rolled(v, -1) for v in w]
                fe = [face(w[c], jnp.where(last_lane, r[(c + 1) % WIDE], r[c]), dgc[j, c]) for c in range(WIDE)]
                r = [rolled(v, 1) for v in fe]
                below = [W[j + 1, c] for c in range(WIDE)]
                for c in range(WIDE):
                    fw = jnp.where(first_lane, r[c - 1], r[c])
                    fs = face(w[c], below[c], dgr[j, c])
                    gain = (fe[c] - fw) + (fs - edge[c])
                    edge[c] = fs
                    ponded = jnp.maximum(w[c] + coef[0, c] * gain + R[h, j, c], 0.0) * L[j, c]
                    s = S[j, c]
                    q = lax.rsqrt(s)
                    intake = jnp.minimum(coef[1, c] + coef[2, c] * (q * q), ponded)
                    W[j, c] = ponded - intake
                    S[j, c] = s + intake
                w = below
            return tuple(edge)

        lax.fori_loop(0, STRIP // ROWS, block, start)

    for c in range(WIDE):
        acc[c] = jnp.zeros((8, LANES), f32)
    for h in range(HOURS):
        lax.fori_loop(0, SUB, lambda i, carry: (substep(h), carry)[1], 0)

        def score(j, carry):
            for c in range(WIDE):
                gap = W[j, c] - O[h, j, c]
                square = gap * gap
                q = lax.rsqrt(1.0 + square)
                acc[c] = acc[c] + own[j, c] * square * (q * q)
            return carry

        lax.fori_loop(0, STRIP, score, 0)

    for src, out in ((W, depth_out), (S, soak_out)):
        for p in range(2):
            def back(j, carry):
                if p == 0:
                    for c in range(CHUNKS):
                        nat[c, pl.ds(j, 8, stride=STRIP), :] = src[j, c]
                else:
                    parts = [rolled(src[j, CHUNKS + k], 64) for k in range(CHUNKS + 1)]
                    for c in range(CHUNKS):
                        nat[c, pl.ds(j, 8, stride=STRIP), :] = jnp.where(lane8 < 64, parts[c], parts[c + 1])
                return carry

            lax.fori_loop(0, STRIP, back, 0)
            for c in range(CHUNKS):
                out[p, 0, :, pl.ds(c * LANES, LANES)] = nat[c, body, :]

    one = jnp.zeros((8, LANES), f32)
    two = jnp.zeros((8, LANES), f32)
    count = jnp.zeros((8, LANES), f32)
    for c in range(WIDE):
        if c < CHUNKS:
            one = one + acc[c]
        else:
            two = two + acc[c]

    def counting(j, total):
        for c in range(CHUNKS):
            total = total + own[j, c]
        return total

    count = lax.fori_loop(0, STRIP, counting, count)
    line = lax.broadcasted_iota(jnp.int32, (8, LANES), 1)
    misfit_out[...] = jnp.where(line == 0, jnp.sum(one), jnp.where(line == 1, jnp.sum(two), jnp.where(line == 2, jnp.sum(count), 0.0)))


VM = pl.BlockSpec(memory_space=pltpu.VMEM)
SM = pl.BlockSpec(memory_space=pltpu.SMEM)


def pack(anc, water, soak, terrain, land, rain):
    i16 = jnp.int16
    return pl.pallas_call(
        pack_kernel,
        out_shape=(
            jax.ShapeDtypeStruct((CY, LANES), i16),
            jax.ShapeDtypeStruct((CY, LANES), i16),
            jax.ShapeDtypeStruct((FIELDS * HALO, CX), i16),
            jax.ShapeDtypeStruct((FIELDS * HALO, CX), i16),
        ),
        in_specs=[SM] + [VM] * 5,
        out_specs=(VM,) * 4,
        scratch_shapes=[pltpu.VMEM((CHUNKS, FIELDS * HALO, LANES), jnp.int32)] * 2,
        name="pack",
    )(anc, water, soak, terrain, land, rain)


def steps(*args):
    f32 = jnp.float32
    wide = pltpu.VMEM((STRIP, WIDE, 8, LANES), f32)
    return pl.pallas_call(
        step_kernel,
        out_shape=(
            jax.ShapeDtypeStruct((2, 1, CY, CX), f32),
            jax.ShapeDtypeStruct((2, 1, CY, CX), f32),
            jax.ShapeDtypeStruct((8, LANES), f32),
        ),
        in_specs=[SM] * 5 + [VM] * 12,
        out_specs=(VM,) * 3,
        scratch_shapes=[
            pltpu.VMEM((CHUNKS + 1, EXT, LANES), f32),
            pltpu.VMEM((EXT, LANES), jnp.int32),
            pltpu.VMEM((EXT, LANES), jnp.int32),
            pltpu.VMEM((2, CHUNKS, FIELDS * HALO, LANES), jnp.int32),
            pltpu.VMEM((STRIP + 1, WIDE, 8, LANES), f32),
            wide, wide, wide, wide, wide,
            pltpu.VMEM((HOURS, STRIP, WIDE, 8, LANES), f32),
            pltpu.VMEM((HOURS, STRIP, WIDE, 8, LANES), f32),
            pltpu.VMEM((3, WIDE, 8, LANES), f32),
            pltpu.VMEM((WIDE, 8, LANES), f32),
        ],
        compiler_params=pltpu.CompilerParams(vmem_limit_bytes=56 << 20),
        name="steps",
    )(*args)


def route(down, right):
    pairs = []
    rows = lax.axis_size("space") // TX
    for r in range(rows):
        for c in range(TX):
            if 0 <= r + down < rows:
                pairs.append((r * TX + c, (r + down) * TX + (c + right) % TX))
    return pairs


def local(water, soak, terrain, land, forcing, seen, cond, suction, manning, owner, anc, prior):
    groups = lax.axis_size("dom")
    tiles = lax.axis_size("space")
    rain = (forcing[:, 0, 0].astype(jnp.float32) - forcing[:, 1, 0].astype(jnp.float32)) * RAIN_SCALE
    rain = rain.astype(jnp.int16)
    rain = lax.all_to_all(jnp.broadcast_to(rain[None], (groups,) + rain.shape), "dom", 0, 0, tiled=True)
    to_west, to_east, to_north, to_south = pack(anc, water, soak, terrain, land, rain)
    from_east = lax.ppermute(to_west, "space", route(0, -1))
    from_west = lax.ppermute(to_east, "space", route(0, 1))
    from_south = lax.ppermute(to_north, "space", route(-1, 0))
    from_north = lax.ppermute(to_south, "space", route(1, 0))
    corner = lambda rows: jnp.concatenate([from_east[rows], from_west[rows]], axis=1)
    corner_south = lax.ppermute(corner(slice(0, 16)), "space", route(-1, 0))
    corner_north = lax.ppermute(corner(slice(CY - 16, CY)), "space", route(1, 0))
    depth, wet, score = steps(anc, owner, cond, suction, manning, water, soak, terrain, land, rain, seen,
                              from_east, from_west, from_north, from_south, corner_north, corner_south)
    lanes = lax.broadcasted_iota(jnp.int32, (1, 1, LANES), 2)
    line = jnp.where(lanes == 3, jnp.mean(prior), score[None, :1])
    line = jnp.broadcast_to(line, (tiles * groups, 1, LANES))
    line = lax.all_to_all(line, ("space", "dom"), 0, 0, tiled=True)
    table = jnp.sum(line.reshape(tiles, groups, LANES), axis=0)
    mean = line.reshape(tiles, groups, LANES)[0, :, 3:4]
    raw = mean * jnp.exp(-SHARPNESS * table[:, :2] / (HOURS * table[:, 2:3]))
    weights = raw / jnp.sum(raw)
    mine = lax.broadcasted_iota(jnp.int32, (groups, 1), 0) == lax.axis_index("dom")
    return depth, wet, jnp.sum(jnp.where(mine, weights, 0.0), axis=0)


def solution(mesh):
    return jax.shard_map(
        local,
        mesh=mesh,
        in_specs=(
            P("dom", "space", None, None),
            P("dom", "space", None, None),
            P("space", None, None),
            P("space", None, None),
            P(None, None, "space", "dom", None),
            P(None, "space", None, None),
            P(),
            P(),
            P(),
            P("dom"),
            P("dom"),
            P("dom"),
        ),
        out_specs=(P("dom", "space", None, None), P("dom", "space", None, None), P("dom")),
        check_vma=False,
    )
```

```python
import jax
import jax.numpy as jnp
from jax import lax
from jax.experimental import pallas as pl
from jax.experimental.pallas import tpu as pltpu
from jax.sharding import PartitionSpec as P

TX = 4
SUB = 6
HOURS = 2
TIME_STEP = 0.01
SLOPE_FLOOR = 0.1
SHARPNESS = 20.0

CY, CX = 256, 512
HALO = SUB * HOURS
COLS = 16
EXT = CY + 2 * HALO
LANES = 128
CHUNKS = CX // LANES
TILES = 7
WIDE = 2 * CHUNKS + 1

RAIN_SCALE = 4096.0
WATER_SCALE = 20000.0
SOAK_SCALE = 16000.0
GROUND_SCALE = 10000.0

FIELDS = 8
ROW_FIELDS = 6
ROW_BLOCK = 80
SHARD = 32
WATER_BODY = -1e30
SCALES = (WATER_SCALE, WATER_SCALE, SOAK_SCALE, SOAK_SCALE, GROUND_SCALE, 1.0, RAIN_SCALE, RAIN_SCALE)
FROM_EAST = (4, 0, 5, 1, 2, 6, 3, 7)
FROM_WEST = (3, 7, 2, 6, 1, 5, 0, 4)


def lane_ids(rows):
    return lax.broadcasted_iota(jnp.int32, (rows, LANES), 1)


def coded(value, scale):
    scaled = value * scale
    return (scaled + jnp.where(scaled >= 0, 0.5, -0.5)).astype(jnp.int32)


def rolled(value, shift, axis=1):
    shift = shift % value.shape[axis]
    return value if shift == 0 else pltpu.roll(value, shift, axis)


def pack_kernel(anc, water, soak, terrain, land, forcing, west_out, east_out, north_out, south_out, rain_out, rows_n, rows_s):
    slots = [anc[p] % 2 for p in range(2)]
    f32 = jnp.float32
    for h in range(HOURS):
        net = forcing[h, 0, 0].astype(f32) - forcing[h, 1, 0].astype(f32)
        rain_out[h] = coded(net, RAIN_SCALE).astype(jnp.int16)

    def part(field, rows, lanes):
        if field < 2:
            return water[slots[field], 0, rows, lanes]
        if field < 4:
            return soak[slots[field - 2], 0, rows, lanes]
        if field == 4:
            return terrain[0, rows, lanes]
        return land[0, rows, lanes].astype(f32)

    first = pl.ds(0, LANES)
    last = pl.ds(CX - LANES, LANES)

    def edges(d, carry):
        rows = pl.ds(pl.multiple_of(d * SHARD, SHARD), SHARD)
        group = lane_ids(SHARD) // COLS
        to_west = jnp.zeros((SHARD, LANES), jnp.int32)
        to_east = jnp.zeros((SHARD, LANES), jnp.int32)
        for f in range(FIELDS):
            if f < ROW_FIELDS:
                a = coded(part(f, rows, first), SCALES[f])
                b = coded(part(f, rows, last), SCALES[f])
            else:
                a = rain_out[f - ROW_FIELDS, :, first].astype(jnp.int32)
                b = rain_out[f - ROW_FIELDS, :, last].astype(jnp.int32)
            at = FROM_EAST[f]
            to_west = jnp.where(group == at, rolled(a, at * COLS), to_west)
            at = FROM_WEST[f]
            to_east = jnp.where(group == at, rolled(b, (at + 1) * COLS - LANES), to_east)
        west_out[rows, :] = to_west.astype(jnp.int16)
        east_out[rows, :] = to_east.astype(jnp.int16)
        return carry

    lax.fori_loop(0, CY // SHARD, edges, 0)

    rest = pl.ds(ROW_FIELDS * HALO, ROW_BLOCK - ROW_FIELDS * HALO)
    for c in range(CHUNKS):
        lanes = pl.ds(c * LANES, LANES)
        for f in range(ROW_FIELDS):
            put = pl.ds(HALO * f, HALO)
            rows_n[c, put, :] = coded(part(f, pl.ds(0, 16), lanes), SCALES[f])[:HALO]
            rows_s[c, put, :] = coded(part(f, pl.ds(CY - 16, 16), lanes), SCALES[f])[16 - HALO:]
        for ref, out in ((rows_n, north_out), (rows_s, south_out)):
            ref[c, rest, :] = jnp.zeros((ROW_BLOCK - ROW_FIELDS * HALO, LANES), jnp.int32)
            out[:, lanes] = ref[c].astype(jnp.int16)


def step_kernel(anc, owner, cond, suction, manning, prior, water, soak, terrain, land, rain, seen,
                east_in, west_in, north_in, south_in, rain_n, rain_s,
                depth_out, soak_out, misfit_out,
                nat, east, west, east_r, west_r, rows_ns, W, S, G, dgc, dgr, L, R, flux, coef):
    f32 = jnp.float32
    slots = [anc[p] % 2 for p in range(2)]
    lane8 = lane_ids(8)
    lane_e = lane_ids(EXT)
    low = lane8 < 64
    last_lane = lane8 == LANES - 1
    first_lane = lane8 == 0
    body = pl.ds(HALO, CY)
    top = pl.ds(0, HALO)
    bottom = pl.ds(HALO + CY, HALO)
    every = pl.ds(0, EXT)

    corners = pl.ds(ROW_BLOCK, 16)
    for ref, of_rain, got, col in ((east, east_r, east_in, 0), (west, west_r, west_in, 1)):
        lanes = pl.ds(col * LANES, LANES)
        ref[body, :] = got[:, :].astype(jnp.int32)
        ref[top, :] = north_in[corners, lanes].astype(jnp.int32)[16 - HALO:]
        ref[bottom, :] = south_in[corners, lanes].astype(jnp.int32)[:HALO]
        early = pl.ds(col * 2 * LANES, LANES)
        late = pl.ds((col * 2 + 1) * LANES, LANES)
        block = pl.ds(2 * SHARD, 16)
        for d in range(CY // SHARD):
            of_rain[pl.ds(HALO + SHARD * d, 16), :] = rain[d, block, early].astype(jnp.int32)
            of_rain[pl.ds(HALO + SHARD * d + 16, 16), :] = rain[d, block, late].astype(jnp.int32)
        of_rain[top, :] = rain_n[pl.ds(32, 16), late].astype(jnp.int32)[16 - HALO:]
        of_rain[bottom, :] = rain_s[pl.ds(32, 16), early].astype(jnp.int32)[:HALO]
    for c in range(CHUNKS):
        lanes = pl.ds(c * LANES, LANES)
        rows_ns[0, c] = north_in[pl.ds(0, ROW_BLOCK), lanes].astype(jnp.int32)
        rows_ns[1, c] = south_in[pl.ds(0, ROW_BLOCK), lanes].astype(jnp.int32)

    def decode(value, f):
        return value.astype(f32) * (1.0 / SCALES[f])

    def tile_rows(dest, f, fix=lambda v: v):
        for c in range(CHUNKS):
            lanes = pl.ds(c * LANES, LANES)
            if f < 2:
                dest[c, body, :] = water[slots[f], 0, :, lanes]
            elif f < 4:
                dest[c, body, :] = soak[slots[f - 2], 0, :, lanes]
            elif f == 4:
                dest[c, body, :] = terrain[0, :, lanes]
            elif f == 5:
                dest[c, body, :] = land[0, :, lanes].astype(f32)
            else:
                h = f - ROW_FIELDS
                for d in range(CY // SHARD):
                    dest[c, pl.ds(HALO + SHARD * d, SHARD), :] = decode(rain[d, pl.ds(SHARD * h, SHARD), lanes].astype(jnp.int32), f)
                dest[c, top, :] = decode(rain_n[pl.ds(16 * h, 16), lanes].astype(jnp.int32)[16 - HALO:], f)
                dest[c, bottom, :] = decode(rain_s[pl.ds(16 * h, 16), lanes].astype(jnp.int32)[:HALO], f)
                continue
            put = pl.ds(HALO * f, HALO)
            dest[c, top, :] = fix(decode(rows_ns[0, c, put, :], f))
            dest[c, bottom, :] = fix(decode(rows_ns[1, c, put, :], f))

    def column_halo(f0, f1, fill, fix=lambda v: v):
        group = lane_e // COLS
        x = jnp.full((EXT, LANES), fill, f32)
        e, w = (east, west) if f0 < ROW_FIELDS else (east_r, west_r)
        for f, ref, table, at in ((f1, e, FROM_EAST, 0), (f0, w, FROM_WEST, 3), (f0, e, FROM_EAST, 4), (f1, w, FROM_WEST, 7)):
            x = jnp.where(group == at, fix(decode(rolled(ref[...], (at - table[f]) * COLS), f)), x)
        nat[CHUNKS] = x

    def tiles(step, per=5):
        def some(i, carry):
            for u in range(per):
                step(pl.multiple_of((i * per + u) * 8, 8))
            return carry

        lax.fori_loop(0, EXT // (8 * per), some, 0)

    def ring(dest, copy, fix=lambda v, c, rows: v):
        def one(at):
            rows = pl.ds(at, 8)
            v = [nat[c, rows, :] for c in range(CHUNKS + 1)]
            if copy:
                for c in range(CHUNKS):
                    dest[c, rows, :] = fix(v[c], c, rows)
            v = [rolled(t, 64) for t in v]
            for k in range(CHUNKS + 1):
                dest[CHUNKS + k, rows, :] = fix(jnp.where(low, v[k - 1], v[k]), CHUNKS + k, rows)

        tiles(one)

    column_halo(0, 1, 0.0)
    tile_rows(W, 0)
    tile_rows(nat, 1)
    ring(W, False)
    guard = lambda v: jnp.maximum(v, 0.1)
    column_halo(2, 3, 1.0, guard)
    tile_rows(S, 2, guard)
    tile_rows(nat, 3, guard)
    ring(S, False)
    column_halo(4, 4, 0.0)
    tile_rows(nat, 4)
    ring(G, True)
    column_halo(5, 5, 0.0)
    tile_rows(nat, 5)
    ring(L, True)
    for h in range(HOURS):
        column_halo(6 + h, 6 + h, 0.0)
        tile_rows(nat, 6 + h)
        ring(R.at[h], True, lambda v, c, rows: jnp.where(L[c, rows, :] > 0.0, v * TIME_STEP, WATER_BODY))
    for c in range(WIDE):
        for ref in (W, G):
            ref[c, pl.ds(EXT, 8), :] = jnp.zeros((8, LANES), f32)
        flux[c, pl.ds(0, 8), :] = jnp.zeros((8, LANES), f32)

    def ground_steps(at):
        rows = pl.ds(at, 8)
        g = [G[c, rows, :] for c in range(WIDE)]
        r = [rolled(v, -1) for v in g]
        for c in range(WIDE):
            dgc[c, rows, :] = jnp.where(last_lane, r[(c + 1) % WIDE], r[c]) - g[c]
            dgr[c, rows, :] = G[c, pl.ds(at + 1, 8), :] - g[c]

    tiles(ground_steps)

    for k in range(3):
        pair = []
        for p in range(2):
            o = owner[slots[p]]
            if k == 0:
                pair.append(jnp.full((8, LANES), TIME_STEP * 0.5 ** (5.0 / 3.0), f32) / jnp.full((8, LANES), manning[o], f32))
            elif k == 1:
                pair.append(jnp.full((8, LANES), TIME_STEP * cond[o], f32))
            else:
                pair.append(jnp.full((8, LANES), TIME_STEP * cond[o] * suction[o], f32))
        for c in range(WIDE):
            v = pair[0] if c < CHUNKS else pair[1]
            if c == CHUNKS:
                v = jnp.where(lane8 < 32, pair[0], pair[1])
            if c == WIDE - 1:
                v = jnp.where(lane8 < 96, pair[1], pair[0])
            coef[k, c] = v

    def face(a, b, dg):
        total = a + b
        slope = (b - a) + dg
        return jnp.exp2(lax.log2(total) * (5.0 / 3.0)) * slope * lax.rsqrt(jnp.abs(slope) + SLOPE_FLOOR)

    def substep(h):
        def one(at):
            rows = pl.ds(at, 8)
            w = [W[c, rows, :] for c in range(WIDE)]
            r = [rolled(v, -1) for v in w]
            fe = [face(w[c], jnp.where(last_lane, r[(c + 1) % WIDE], r[c]), dgc[c, rows, :]) for c in range(WIDE)]
            r = [rolled(v, 1) for v in fe]
            for c in range(WIDE):
                fw = jnp.where(first_lane, r[c - 1], r[c])
                fs = face(w[c], W[c, pl.ds(at + 1, 8), :], dgr[c, rows, :])
                flux[c, pl.ds(at + 8, 8), :] = fs
                gain = (fe[c] - fw) + (fs - flux[c, pl.ds(at + 7, 8), :])
                ponded = jnp.maximum(w[c] + coef[0, c] * gain + R[h, c, rows, :], 0.0)
                s = S[c, rows, :]
                intake = jnp.minimum(coef[1, c] + coef[2, c] / s, ponded)
                W[c, rows, :] = ponded - intake
                S[c, rows, :] = s + intake

        tiles(one, TILES)

    def slot_one(ref, rows):
        v = [rolled(ref[CHUNKS + k, rows, :], 64) for k in range(CHUNKS + 1)]
        return [jnp.where(low, v[k], v[k + 1]) for k in range(CHUNKS)]

    def hour(h, total):
        lax.fori_loop(0, SUB, lambda i, carry: (substep(h), carry)[1], 0)

        def score(i, total):
            total = list(total)
            for half in range(2):
                start = pl.multiple_of(i * 16, 16)
                rows = pl.ds(start + half * 8, 8)
                inner = pl.ds(start + half * 8 + HALO, 8)
                ones = slot_one(W, inner)
                for c in range(CHUNKS):
                    lanes = pl.ds(c * LANES, LANES)
                    o = seen[h, 0, pl.ds(start, 16), lanes].astype(f32)[half * 8:half * 8 + 8]
                    keep = land[0, rows, lanes].astype(f32)
                    total[2] = total[2] + keep
                    for p, v in enumerate((W[c, inner, :], ones[c])):
                        depth_out[p, 0, rows, lanes] = v
                        gap = v - o
                        square = gap * gap
                        total[p] = total[p] + keep * square / (1.0 + square)
            return tuple(total)

        return lax.fori_loop(0, CY // 16, score, total)

    zero = jnp.zeros((8, LANES), f32)
    one, two, cells = lax.fori_loop(0, HOURS, hour, (zero, zero, zero))

    def wet(i, carry):
        for u in range(4):
            start = pl.multiple_of((i * 4 + u) * 8, 8)
            rows = pl.ds(start, 8)
            inner = pl.ds(start + HALO, 8)
            ones = slot_one(S, inner)
            for c in range(CHUNKS):
                lanes = pl.ds(c * LANES, LANES)
                soak_out[0, 0, rows, lanes] = S[c, inner, :]
                soak_out[1, 0, rows, lanes] = ones[c]
        return carry

    lax.fori_loop(0, CY // 32, wet, 0)
    line = lane_ids(1)
    misfit_out[...] = jnp.where(
        line == 0,
        jnp.sum(one),
        jnp.where(line == 1, jnp.sum(two), jnp.where(line == 2, jnp.sum(cells), (prior[0] + prior[1]) * 0.5)),
    )


VM = pl.BlockSpec(memory_space=pltpu.VMEM)
SM = pl.BlockSpec(memory_space=pltpu.SMEM)


def pack(anc, water, soak, terrain, land, forcing):
    i16 = jnp.int16
    return pl.pallas_call(
        pack_kernel,
        out_shape=(
            jax.ShapeDtypeStruct((CY, LANES), i16),
            jax.ShapeDtypeStruct((CY, LANES), i16),
            jax.ShapeDtypeStruct((ROW_BLOCK, CX), i16),
            jax.ShapeDtypeStruct((ROW_BLOCK, CX), i16),
            jax.ShapeDtypeStruct((HOURS, SHARD, CX), i16),
        ),
        in_specs=[SM] + [VM] * 5,
        out_specs=(VM,) * 5,
        scratch_shapes=[pltpu.VMEM((CHUNKS, ROW_BLOCK, LANES), jnp.int32)] * 2,
        name="pack",
    )(anc, water, soak, terrain, land, forcing)


def steps(*args):
    f32 = jnp.float32
    wide = pltpu.VMEM((WIDE, EXT, LANES), f32)
    tall = pltpu.VMEM((WIDE, EXT + 8, LANES), f32)
    return pl.pallas_call(
        step_kernel,
        out_shape=(
            jax.ShapeDtypeStruct((2, 1, CY, CX), f32),
            jax.ShapeDtypeStruct((2, 1, CY, CX), f32),
            jax.ShapeDtypeStruct((1, LANES), f32),
        ),
        in_specs=[SM] * 6 + [VM] * 12,
        out_specs=(VM,) * 3,
        scratch_shapes=[
            pltpu.VMEM((CHUNKS + 1, EXT, LANES), f32),
            pltpu.VMEM((EXT, LANES), jnp.int32),
            pltpu.VMEM((EXT, LANES), jnp.int32),
            pltpu.VMEM((EXT, LANES), jnp.int32),
            pltpu.VMEM((EXT, LANES), jnp.int32),
            pltpu.VMEM((2, CHUNKS, ROW_BLOCK, LANES), jnp.int32),
            tall, wide, tall, wide, wide, wide,
            pltpu.VMEM((HOURS, WIDE, EXT, LANES), f32),
            tall,
            pltpu.VMEM((3, WIDE, 8, LANES), f32),
        ],
        compiler_params=pltpu.CompilerParams(vmem_limit_bytes=40 << 20),
        name="steps",
    )(*args)


def route(down, right):
    pairs = []
    rows = lax.axis_size("space") // TX
    for r in range(rows):
        for c in range(TX):
            if 0 <= r + down < rows:
                pairs.append((r * TX + c, (r + down) * TX + (c + right) % TX))
    return pairs


def local(water, soak, terrain, land, forcing, seen, cond, suction, manning, owner, anc, prior):
    groups = lax.axis_size("dom")
    tiles = lax.axis_size("space")
    to_west, to_east, to_north, to_south, rain = pack(anc, water, soak, terrain, land, forcing)
    from_east = lax.ppermute(to_west, "space", route(0, -1))
    from_west = lax.ppermute(to_east, "space", route(0, 1))

    shard = jnp.concatenate([from_east[:16], from_east[16:32], from_west[:16], from_west[16:32]], axis=1)
    shard = jnp.concatenate([rain.reshape(HOURS * SHARD, CX), shard], axis=0)
    rain = lax.all_to_all(jnp.broadcast_to(shard[None], (groups,) + shard.shape), "dom", 0, 0, tiled=True)

    def with_corners(fields, rows):
        corner = jnp.concatenate([from_east[rows], from_west[rows]] * 2, axis=1)
        return jnp.concatenate([fields, corner], axis=0)

    from_south = lax.ppermute(with_corners(to_north, slice(0, 16)), "space", route(-1, 0))
    from_north = lax.ppermute(with_corners(to_south, slice(CY - 16, CY)), "space", route(1, 0))

    top = jnp.concatenate([rain[0, 0:16], rain[0, 32:48], rain[0, 64:80]], axis=0)
    bottom = jnp.concatenate([rain[-1, 16:32], rain[-1, 48:64], rain[-1, 64:80]], axis=0)
    rain_south = lax.ppermute(top, "space", route(-1, 0))
    rain_north = lax.ppermute(bottom, "space", route(1, 0))

    depth, wet, score = steps(anc, owner, cond, suction, manning, prior, water, soak, terrain, land, rain, seen,
                              from_east, from_west, from_north, from_south, rain_north, rain_south)

    score = score + lax.ppermute(score, "space", [(i, i ^ 1) for i in range(tiles)])
    peers = [[t * groups + d for t in range(k, tiles, 2) for d in range(groups)] for k in range(2)]
    line = jnp.broadcast_to(score[None], (tiles // 2 * groups, 1, LANES))
    line = lax.all_to_all(line, ("space", "dom"), 0, 0, axis_index_groups=peers, tiled=True)
    line = line.reshape(tiles // 2, groups, LANES)
    table = jnp.sum(line, axis=0)
    raw = 0.5 * line[0, :, 3:4] * jnp.exp(-SHARPNESS * table[:, :2] / table[:, 2:3])
    weights = raw / jnp.sum(raw)
    mine = lax.broadcasted_iota(jnp.int32, (groups, 1), 0) == lax.axis_index("dom")
    return depth, wet, jnp.sum(jnp.where(mine, weights, 0.0), axis=0)


def solution(mesh):
    return jax.shard_map(
        local,
        mesh=mesh,
        in_specs=(
            P("dom", "space", None, None),
            P("dom", "space", None, None),
            P("space", None, None),
            P("space", None, None),
            P(None, None, "space", "dom", None),
            P(None, "space", None, None),
            P(),
            P(),
            P(),
            P("dom"),
            P("dom"),
            P("dom"),
        ),
        out_specs=(P("dom", "space", None, None), P("dom", "space", None, None), P("dom")),
        check_vma=False,
    )
```

```python
import jax
import jax.numpy as jnp
from jax import lax
from jax.experimental import pallas as pl
from jax.experimental.pallas import tpu as pltpu
from jax.sharding import PartitionSpec as P


TX = 4
SUB = 6
HOURS = 2
TIME_STEP = 0.01
SLOPE_FLOOR = 0.1
SHARPNESS = 20.0

CY, CX = 256, 512
HALO = SUB * HOURS
COLS = 16
EXT = CY + 2 * HALO
LANES = 128
CHUNKS = CX // LANES
TILES = 7
WIDE = 2 * CHUNKS + 1

RAIN_SCALE = 4096.0
WATER_SCALE = 20000.0
SOAK_SCALE = 16000.0
GROUND_SCALE = 10000.0

FIELDS = 8
ROW_FIELDS = 6
ROW_BLOCK = 80
SHARD = 32
WATER_BODY = -1e30
SCALES = (WATER_SCALE, WATER_SCALE, SOAK_SCALE, SOAK_SCALE, GROUND_SCALE, 1.0, RAIN_SCALE, RAIN_SCALE)
FROM_EAST = (4, 0, 5, 1, 2, 6, 3, 7)
FROM_WEST = (3, 7, 2, 6, 1, 5, 0, 4)


def lane_ids(rows):
    return lax.broadcasted_iota(jnp.int32, (rows, LANES), 1)


def coded(value, scale):
    scaled = value * scale
    return (scaled + jnp.where(scaled >= 0, 0.5, -0.5)).astype(jnp.int32)


def rolled(value, shift, axis=1):
    shift = shift % value.shape[axis]
    return value if shift == 0 else pltpu.roll(value, shift, axis)


def field_part(refs, slots, field, rows, lanes):
    water, soak, terrain, land = refs
    if field < 2:
        return water[slots[field], 0, rows, lanes]
    if field < 4:
        return soak[slots[field - 2], 0, rows, lanes]
    if field == 4:
        return terrain[0, rows, lanes]
    return land[0, rows, lanes].astype(jnp.float32)


def columns_kernel(anc, *refs):
    first, last = refs[:4], refs[4:8]
    forcing, west_out, east_out, rain_out = refs[8:]
    slots = [anc[p] % 2 for p in range(2)]
    every = pl.ds(0, LANES)
    for h in range(HOURS):
        net = forcing[h, 0, 0].astype(jnp.float32) - forcing[h, 1, 0].astype(jnp.float32)
        rain_out[h] = coded(net, RAIN_SCALE).astype(jnp.int16)

    def edges(d, carry):
        rows = pl.ds(pl.multiple_of(d * SHARD, SHARD), SHARD)
        group = lane_ids(SHARD) // COLS
        to_west = jnp.zeros((SHARD, LANES), jnp.int32)
        to_east = jnp.zeros((SHARD, LANES), jnp.int32)
        for f in range(FIELDS):
            if f < ROW_FIELDS:
                a = coded(field_part(first, slots, f, rows, every), SCALES[f])
                b = coded(field_part(last, slots, f, rows, every), SCALES[f])
            else:
                a = rain_out[f - ROW_FIELDS, :, pl.ds(0, LANES)].astype(jnp.int32)
                b = rain_out[f - ROW_FIELDS, :, pl.ds(CX - LANES, LANES)].astype(jnp.int32)
            at = FROM_EAST[f]
            to_west = jnp.where(group == at, rolled(a, at * COLS), to_west)
            at = FROM_WEST[f]
            to_east = jnp.where(group == at, rolled(b, (at + 1) * COLS - LANES), to_east)
        west_out[rows, :] = to_west.astype(jnp.int16)
        east_out[rows, :] = to_east.astype(jnp.int16)
        return carry

    lax.fori_loop(0, CY // SHARD, edges, 0)


def rows_kernel(anc, *refs):
    first, last = refs[:4], refs[4:8]
    north_out, south_out, rows_n, rows_s = refs[8:]
    slots = [anc[p] % 2 for p in range(2)]
    rest = pl.ds(ROW_FIELDS * HALO, ROW_BLOCK - ROW_FIELDS * HALO)
    sixteen = pl.ds(0, 16)
    for c in range(CHUNKS):
        lanes = pl.ds(c * LANES, LANES)
        for f in range(ROW_FIELDS):
            put = pl.ds(HALO * f, HALO)
            rows_n[c, put, :] = coded(field_part(first, slots, f, sixteen, lanes), SCALES[f])[:HALO]
            rows_s[c, put, :] = coded(field_part(last, slots, f, sixteen, lanes), SCALES[f])[16 - HALO:]
        for ref, out in ((rows_n, north_out), (rows_s, south_out)):
            ref[c, rest, :] = jnp.zeros((ROW_BLOCK - ROW_FIELDS * HALO, LANES), jnp.int32)
            out[:, lanes] = ref[c].astype(jnp.int16)


def step_kernel(anc, owner, cond, suction, manning, prior, water_in, soak_in, terrain_in, land_in, rain_in, seen_in,
                east_in, west_in, north_in, south_in, rain_n, rain_s,
                depth_out, soak_out, misfit_out,
                water, soak, terrain, land, rain, seen, sems,
                nat, east, west, east_r, west_r, rows_ns, W, S, G, dgc, dgr, L, R, flux, coef):
    f32 = jnp.float32
    sources = (water_in, soak_in, terrain_in, land_in, rain_in, seen_in)
    copies = [
        pltpu.make_async_copy(src, dst, sems.at[i])
        for i, (src, dst) in enumerate(zip(sources, (water, soak, terrain, land, rain, seen)))
    ]
    for copy in copies:
        copy.start()
    slots = [anc[p] % 2 for p in range(2)]
    lane8 = lane_ids(8)
    lane_e = lane_ids(EXT)
    low = lane8 < 64
    last_lane = lane8 == LANES - 1
    first_lane = lane8 == 0
    body = pl.ds(HALO, CY)
    top = pl.ds(0, HALO)
    bottom = pl.ds(HALO + CY, HALO)
    every = pl.ds(0, EXT)

    corners = pl.ds(ROW_BLOCK, 16)
    for ref, of_rain, got, col in ((east, east_r, east_in, 0), (west, west_r, west_in, 1)):
        lanes = pl.ds(col * LANES, LANES)
        ref[body, :] = got[:, :].astype(jnp.int32)
        ref[top, :] = north_in[corners, lanes].astype(jnp.int32)[16 - HALO:]
        ref[bottom, :] = south_in[corners, lanes].astype(jnp.int32)[:HALO]
        early = pl.ds(col * 2 * LANES, LANES)
        late = pl.ds((col * 2 + 1) * LANES, LANES)
        of_rain[top, :] = rain_n[pl.ds(32, 16), late].astype(jnp.int32)[16 - HALO:]
        of_rain[bottom, :] = rain_s[pl.ds(32, 16), early].astype(jnp.int32)[:HALO]
    for c in range(CHUNKS):
        lanes = pl.ds(c * LANES, LANES)
        rows_ns[0, c] = north_in[pl.ds(0, ROW_BLOCK), lanes].astype(jnp.int32)
        rows_ns[1, c] = south_in[pl.ds(0, ROW_BLOCK), lanes].astype(jnp.int32)

    def decode(value, f):
        return value.astype(f32) * (1.0 / SCALES[f])

    def tile_rows(dest, f, fix=lambda v: v):
        for c in range(CHUNKS):
            lanes = pl.ds(c * LANES, LANES)
            if f < 2:
                dest[c, body, :] = water[slots[f], 0, :, lanes]
            elif f < 4:
                dest[c, body, :] = soak[slots[f - 2], 0, :, lanes]
            elif f == 4:
                dest[c, body, :] = terrain[0, :, lanes]
            elif f == 5:
                dest[c, body, :] = land[0, :, lanes].astype(f32)
            else:
                h = f - ROW_FIELDS
                for d in range(CY // SHARD):
                    dest[c, pl.ds(HALO + SHARD * d, SHARD), :] = decode(rain[d % 4, d // 4, pl.ds(SHARD * h, SHARD), lanes].astype(jnp.int32), f)
                dest[c, top, :] = decode(rain_n[pl.ds(16 * h, 16), lanes].astype(jnp.int32)[16 - HALO:], f)
                dest[c, bottom, :] = decode(rain_s[pl.ds(16 * h, 16), lanes].astype(jnp.int32)[:HALO], f)
                continue
            put = pl.ds(HALO * f, HALO)
            dest[c, top, :] = fix(decode(rows_ns[0, c, put, :], f))
            dest[c, bottom, :] = fix(decode(rows_ns[1, c, put, :], f))

    def column_halo(f0, f1, fill, fix=lambda v: v):
        group = lane_e // COLS
        x = jnp.full((EXT, LANES), fill, f32)
        e, w = (east, west) if f0 < ROW_FIELDS else (east_r, west_r)
        for f, ref, table, at in ((f1, e, FROM_EAST, 0), (f0, w, FROM_WEST, 3), (f0, e, FROM_EAST, 4), (f1, w, FROM_WEST, 7)):
            x = jnp.where(group == at, fix(decode(rolled(ref[...], (at - table[f]) * COLS), f)), x)
        nat[CHUNKS] = x

    def tiles(step, per=5):
        def some(i, carry):
            for u in range(per):
                step(pl.multiple_of((i * per + u) * 8, 8))
            return carry

        lax.fori_loop(0, EXT // (8 * per), some, 0)

    def ring(dest, copy, fix=lambda v, c, rows: v):
        def one(at):
            rows = pl.ds(at, 8)
            v = [nat[c, rows, :] for c in range(CHUNKS + 1)]
            if copy:
                for c in range(CHUNKS):
                    dest[c, rows, :] = fix(v[c], c, rows)
            v = [rolled(t, 64) for t in v]
            for k in range(CHUNKS + 1):
                dest[CHUNKS + k, rows, :] = fix(jnp.where(low, v[k - 1], v[k]), CHUNKS + k, rows)

        tiles(one)

    column_halo(0, 1, 0.0)
    copies[0].wait()
    tile_rows(W, 0)
    tile_rows(nat, 1)
    ring(W, False)
    guard = lambda v: jnp.maximum(v, 0.1)
    column_halo(2, 3, 1.0, guard)
    copies[1].wait()
    tile_rows(S, 2, guard)
    tile_rows(nat, 3, guard)
    ring(S, False)
    column_halo(4, 4, 0.0)
    copies[2].wait()
    tile_rows(nat, 4)
    ring(G, True)
    column_halo(5, 5, 0.0)
    copies[3].wait()
    tile_rows(nat, 5)
    ring(L, True)
    copies[4].wait()
    for of_rain, col in ((east_r, 0), (west_r, 1)):
        for d in range(CY // SHARD):
            for half in range(2):
                lanes = pl.ds((col * 2 + half) * LANES, LANES)
                part = rain[d % 4, d // 4, pl.ds(2 * SHARD, 16), lanes]
                of_rain[pl.ds(HALO + SHARD * d + 16 * half, 16), :] = part.astype(jnp.int32)
    for h in range(HOURS):
        column_halo(6 + h, 6 + h, 0.0)
        tile_rows(nat, 6 + h)
        ring(R.at[h], True, lambda v, c, rows: jnp.where(L[c, rows, :] > 0.0, v * TIME_STEP, WATER_BODY))
    for c in range(WIDE):
        for ref in (W, G):
            ref[c, pl.ds(EXT, 8), :] = jnp.zeros((8, LANES), f32)
        flux[c, pl.ds(0, 8), :] = jnp.zeros((8, LANES), f32)

    def ground_steps(at):
        rows = pl.ds(at, 8)
        g = [G[c, rows, :] for c in range(WIDE)]
        r = [rolled(v, -1) for v in g]
        for c in range(WIDE):
            dgc[c, rows, :] = jnp.where(last_lane, r[(c + 1) % WIDE], r[c]) - g[c]
            dgr[c, rows, :] = G[c, pl.ds(at + 1, 8), :] - g[c]

    tiles(ground_steps)

    for k in range(3):
        pair = []
        for p in range(2):
            o = owner[slots[p]]
            if k == 0:
                pair.append(jnp.full((8, LANES), TIME_STEP * 0.5 ** (5.0 / 3.0), f32) / jnp.full((8, LANES), manning[o], f32))
            elif k == 1:
                pair.append(jnp.full((8, LANES), TIME_STEP * cond[o], f32))
            else:
                pair.append(jnp.full((8, LANES), TIME_STEP * cond[o] * suction[o], f32))
        for c in range(WIDE):
            v = pair[0] if c < CHUNKS else pair[1]
            if c == CHUNKS:
                v = jnp.where(lane8 < 32, pair[0], pair[1])
            if c == WIDE - 1:
                v = jnp.where(lane8 < 96, pair[1], pair[0])
            coef[k, c] = v

    def face(a, b, dg):
        total = a + b
        slope = (b - a) + dg
        return jnp.exp2(lax.log2(total) * (5.0 / 3.0)) * slope * lax.rsqrt(jnp.abs(slope) + SLOPE_FLOOR)

    def substep(h):
        def one(at):
            rows = pl.ds(at, 8)
            w = [W[c, rows, :] for c in range(WIDE)]
            r = [rolled(v, -1) for v in w]
            fe = [face(w[c], jnp.where(last_lane, r[(c + 1) % WIDE], r[c]), dgc[c, rows, :]) for c in range(WIDE)]
            r = [rolled(v, 1) for v in fe]
            for c in range(WIDE):
                fw = jnp.where(first_lane, r[c - 1], r[c])
                fs = face(w[c], W[c, pl.ds(at + 1, 8), :], dgr[c, rows, :])
                flux[c, pl.ds(at + 8, 8), :] = fs
                gain = (fe[c] - fw) + (fs - flux[c, pl.ds(at + 7, 8), :])
                ponded = jnp.maximum(w[c] + coef[0, c] * gain + R[h, c, rows, :], 0.0)
                s = S[c, rows, :]
                intake = jnp.minimum(coef[1, c] + coef[2, c] / s, ponded)
                W[c, rows, :] = ponded - intake
                S[c, rows, :] = s + intake

        tiles(one, TILES)

    def slot_one(ref, rows):
        v = [rolled(ref[CHUNKS + k, rows, :], 64) for k in range(CHUNKS + 1)]
        return [jnp.where(low, v[k], v[k + 1]) for k in range(CHUNKS)]

    def hour(h, total):
        lax.fori_loop(0, SUB, lambda i, carry: (substep(h), carry)[1], 0)

        def score(i, total):
            total = list(total)
            for half in range(2):
                start = pl.multiple_of(i * 16, 16)
                rows = pl.ds(start + half * 8, 8)
                inner = pl.ds(start + half * 8 + HALO, 8)
                ones = slot_one(W, inner)
                for c in range(CHUNKS):
                    lanes = pl.ds(c * LANES, LANES)
                    o = seen[h, 0, pl.ds(start, 16), lanes].astype(f32)[half * 8:half * 8 + 8]
                    keep = land[0, rows, lanes].astype(f32)
                    total[2] = total[2] + keep
                    for p, v in enumerate((W[c, inner, :], ones[c])):
                        depth_out[p, 0, rows, lanes] = v
                        gap = v - o
                        square = gap * gap
                        total[p] = total[p] + keep * square / (1.0 + square)
            return tuple(total)

        return lax.fori_loop(0, CY // 16, score, total)

    copies[5].wait()
    zero = jnp.zeros((8, LANES), f32)
    one, two, cells = lax.fori_loop(0, HOURS, hour, (zero, zero, zero))

    def wet(i, carry):
        for u in range(4):
            start = pl.multiple_of((i * 4 + u) * 8, 8)
            rows = pl.ds(start, 8)
            inner = pl.ds(start + HALO, 8)
            ones = slot_one(S, inner)
            for c in range(CHUNKS):
                lanes = pl.ds(c * LANES, LANES)
                soak_out[0, 0, rows, lanes] = S[c, inner, :]
                soak_out[1, 0, rows, lanes] = ones[c]
        return carry

    lax.fori_loop(0, CY // 32, wet, 0)
    line = lane_ids(1)
    misfit_out[...] = jnp.where(
        line == 0,
        jnp.sum(one),
        jnp.where(line == 1, jnp.sum(two), jnp.where(line == 2, jnp.sum(cells), (prior[0] + prior[1]) * 0.5)),
    )


VM = pl.BlockSpec(memory_space=pltpu.VMEM)
SM = pl.BlockSpec(memory_space=pltpu.SMEM)


def ends(shape, where):
    pair = pl.BlockSpec((2, 1) + shape, lambda i: (0, 0) + where)
    one = pl.BlockSpec((1,) + shape, lambda i: (0,) + where)
    return [pair, pair, one, one]


def whole(shape):
    return pl.BlockSpec(shape, lambda i: (0,) * len(shape))


def pack_columns(anc, fields, forcing):
    shapes = [(CY, LANES), (CY, LANES), (HOURS, SHARD, CX)]
    return pl.pallas_call(
        columns_kernel,
        out_shape=[jax.ShapeDtypeStruct(shape, jnp.int16) for shape in shapes],
        grid=(1,),
        in_specs=[SM] + ends((CY, LANES), (0, 0)) + ends((CY, LANES), (0, CHUNKS - 1)) + [whole(forcing.shape)],
        out_specs=[whole(shape) for shape in shapes],
        name="pack_columns",
    )(anc, *fields, *fields, forcing)


def pack_rows(anc, fields):
    shape = (ROW_BLOCK, CX)
    return pl.pallas_call(
        rows_kernel,
        out_shape=[jax.ShapeDtypeStruct(shape, jnp.int16)] * 2,
        grid=(1,),
        in_specs=[SM] + ends((16, CX), (0, 0)) + ends((16, CX), (CY // 16 - 1, 0)),
        out_specs=[whole(shape)] * 2,
        scratch_shapes=[pltpu.VMEM((CHUNKS, ROW_BLOCK, LANES), jnp.int32)] * 2,
        name="pack_rows",
    )(anc, *fields, *fields)


def steps(*args):
    f32 = jnp.float32
    wide = pltpu.VMEM((WIDE, EXT, LANES), f32)
    tall = pltpu.VMEM((WIDE, EXT + 8, LANES), f32)
    return pl.pallas_call(
        step_kernel,
        out_shape=(
            jax.ShapeDtypeStruct((2, 1, CY, CX), f32),
            jax.ShapeDtypeStruct((2, 1, CY, CX), f32),
            jax.ShapeDtypeStruct((1, LANES), f32),
        ),
        in_specs=[SM] * 6 + [pl.BlockSpec(memory_space=pltpu.HBM)] * 6 + [VM] * 6,
        out_specs=(VM,) * 3,
        scratch_shapes=[pltpu.VMEM(x.shape, x.dtype) for x in args[6:12]]
        + [
            pltpu.SemaphoreType.DMA((6,)),
            pltpu.VMEM((CHUNKS + 1, EXT, LANES), f32),
            pltpu.VMEM((EXT, LANES), jnp.int32),
            pltpu.VMEM((EXT, LANES), jnp.int32),
            pltpu.VMEM((EXT, LANES), jnp.int32),
            pltpu.VMEM((EXT, LANES), jnp.int32),
            pltpu.VMEM((2, CHUNKS, ROW_BLOCK, LANES), jnp.int32),
            tall, wide, tall, wide, wide, wide,
            pltpu.VMEM((HOURS, WIDE, EXT, LANES), f32),
            tall,
            pltpu.VMEM((3, WIDE, 8, LANES), f32),
        ],
        compiler_params=pltpu.CompilerParams(vmem_limit_bytes=40 << 20),
        name="steps",
    )(*args)


def route(down, right):
    pairs = []
    rows = lax.axis_size("space") // TX
    for r in range(rows):
        for c in range(TX):
            if 0 <= r + down < rows:
                pairs.append((r * TX + c, (r + down) * TX + (c + right) % TX))
    return pairs


def window(water, soak, terrain, land, forcing, seen, cond, suction, manning, owner, anc, prior):
    groups = lax.axis_size("dom")
    tiles = lax.axis_size("space")
    fields = (water, soak, terrain, land)
    to_west, to_east, rain = pack_columns(anc, fields, forcing)
    from_east = lax.ppermute(to_west, "space", route(0, -1))
    from_west = lax.ppermute(to_east, "space", route(0, 1))
    to_north, to_south = pack_rows(anc, fields)

    shard = jnp.concatenate([from_east[:16], from_east[16:32], from_west[:16], from_west[16:32]], axis=1)
    shard = jnp.concatenate([rain.reshape(HOURS * SHARD, CX), shard], axis=0)
    line = groups // 2
    partner = lax.ppermute(shard, "dom", [(i, (i + line) % groups) for i in range(groups)])

    def with_corners(block, rows):
        corner = jnp.concatenate([from_east[rows], from_west[rows]] * 2, axis=1)
        return jnp.concatenate([block, corner], axis=0)

    from_south = lax.ppermute(with_corners(to_north, slice(0, 16)), "space", route(-1, 0))
    from_north = lax.ppermute(with_corners(to_south, slice(CY - 16, CY)), "space", route(1, 0))
    upper = lax.axis_index("dom") >= line
    pair = jnp.stack([jnp.where(upper, partner, shard), jnp.where(upper, shard, partner)])
    lines = [list(range(line)), list(range(line, groups))]
    rain = lax.all_to_all(jnp.broadcast_to(pair[None], (line,) + pair.shape), "dom", 0, 0, axis_index_groups=lines, tiled=True)

    a, b = rain[0, 0], rain[-1, -1]
    rain_south = lax.ppermute(jnp.concatenate([a[0:16], a[32:48], a[64:80]], axis=0), "space", route(-1, 0))
    rain_north = lax.ppermute(jnp.concatenate([b[16:32], b[48:64], b[64:80]], axis=0), "space", route(1, 0))

    depth, wet, score = steps(anc, owner, cond, suction, manning, prior, water, soak, terrain, land, rain, seen,
                              from_east, from_west, from_north, from_south, rain_north, rain_south)

    score = score + lax.ppermute(score, "space", [(i, i ^ 1) for i in range(tiles)])
    peers = [[t * groups + d for t in range(k, tiles, 2) for d in range(groups)] for k in range(2)]
    line = jnp.broadcast_to(score[None], (tiles // 2 * groups, 1, LANES))
    line = lax.all_to_all(line, ("space", "dom"), 0, 0, axis_index_groups=peers, tiled=True)
    line = line.reshape(tiles // 2, groups, LANES)
    table = jnp.sum(line, axis=0)
    raw = 0.5 * line[0, :, 3:4] * jnp.exp(-SHARPNESS * table[:, :2] / table[:, 2:3])
    weights = raw / jnp.sum(raw)
    mine = lax.broadcasted_iota(jnp.int32, (groups, 1), 0) == lax.axis_index("dom")
    return depth, wet, jnp.sum(jnp.where(mine, weights, 0.0), axis=0)


def solution(mesh):
    return jax.shard_map(
        window,
        mesh=mesh,
        in_specs=(
            P("dom", "space", None, None),
            P("dom", "space", None, None),
            P("space", None, None),
            P("space", None, None),
            P(None, None, "space", "dom", None),
            P(None, "space", None, None),
            P(),
            P(),
            P(),
            P("dom"),
            P("dom"),
            P("dom"),
        ),
        out_specs=(P("dom", "space", None, None), P("dom", "space", None, None), P("dom")),
        check_vma=False,
    )
```

```python
import jax
import jax.numpy as jnp
from jax import lax
from jax.experimental import pallas as pl
from jax.experimental.pallas import tpu as pltpu
from jax.sharding import PartitionSpec as P


TX = 4
SUB = 6
HOURS = 2
TIME_STEP = 0.01
SLOPE_FLOOR = 0.1
SHARPNESS = 20.0

CY, CX = 256, 512
HALO = SUB * HOURS
COLS = 16
EXT = CY + 2 * HALO
LANES = 128
CHUNKS = CX // LANES
TILES = 7
WIDE = 2 * CHUNKS + 1

RAIN_SCALE = 4096.0
WATER_SCALE = 20000.0
SOAK_SCALE = 16000.0
GROUND_SCALE = 10000.0

FIELDS = 8
ROW_FIELDS = 6
ROW_BLOCK = 80
SHARD = 32
WATER_BODY = -1e30
SCALES = (WATER_SCALE, WATER_SCALE, SOAK_SCALE, SOAK_SCALE, GROUND_SCALE, 1.0, RAIN_SCALE, RAIN_SCALE)
FROM_EAST = (4, 0, 5, 1, 2, 6, 3, 7)
FROM_WEST = (3, 7, 2, 6, 1, 5, 0, 4)


def lane_ids(rows):
    return lax.broadcasted_iota(jnp.int32, (rows, LANES), 1)


def coded(value, scale):
    scaled = value * scale
    return (scaled + jnp.where(scaled >= 0, 0.5, -0.5)).astype(jnp.int32)


def rolled(value, shift, axis=1):
    shift = shift % value.shape[axis]
    return value if shift == 0 else pltpu.roll(value, shift, axis)


def field_part(refs, slots, field, rows, lanes):
    water, soak, terrain, land = refs
    if field < 2:
        return water[slots[field], 0, rows, lanes]
    if field < 4:
        return soak[slots[field - 2], 0, rows, lanes]
    if field == 4:
        return terrain[0, rows, lanes]
    return land[0, rows, lanes].astype(jnp.float32)


def columns_kernel(anc, *refs):
    first, last = refs[:4], refs[4:8]
    forcing, west_out, east_out, rain_out = refs[8:]
    slots = [anc[p] % 2 for p in range(2)]
    every = pl.ds(0, LANES)
    for h in range(HOURS):
        net = forcing[h, 0, 0].astype(jnp.float32) - forcing[h, 1, 0].astype(jnp.float32)
        rain_out[h] = coded(net, RAIN_SCALE).astype(jnp.int16)

    def edges(d, carry):
        rows = pl.ds(pl.multiple_of(d * SHARD, SHARD), SHARD)
        group = lane_ids(SHARD) // COLS
        to_west = jnp.zeros((SHARD, LANES), jnp.int32)
        to_east = jnp.zeros((SHARD, LANES), jnp.int32)
        for f in range(FIELDS):
            if f < ROW_FIELDS:
                a = coded(field_part(first, slots, f, rows, every), SCALES[f])
                b = coded(field_part(last, slots, f, rows, every), SCALES[f])
            else:
                a = rain_out[f - ROW_FIELDS, :, pl.ds(0, LANES)].astype(jnp.int32)
                b = rain_out[f - ROW_FIELDS, :, pl.ds(CX - LANES, LANES)].astype(jnp.int32)
            at = FROM_EAST[f]
            to_west = jnp.where(group == at, rolled(a, at * COLS), to_west)
            at = FROM_WEST[f]
            to_east = jnp.where(group == at, rolled(b, (at + 1) * COLS - LANES), to_east)
        west_out[rows, :] = to_west.astype(jnp.int16)
        east_out[rows, :] = to_east.astype(jnp.int16)
        return carry

    lax.fori_loop(0, CY // SHARD, edges, 0)


def rows_kernel(anc, *refs):
    first, last = refs[:4], refs[4:8]
    north_out, south_out, rows_n, rows_s = refs[8:]
    slots = [anc[p] % 2 for p in range(2)]
    rest = pl.ds(ROW_FIELDS * HALO, ROW_BLOCK - ROW_FIELDS * HALO)
    sixteen = pl.ds(0, 16)
    for c in range(CHUNKS):
        lanes = pl.ds(c * LANES, LANES)
        for f in range(ROW_FIELDS):
            put = pl.ds(HALO * f, HALO)
            rows_n[c, put, :] = coded(field_part(first, slots, f, sixteen, lanes), SCALES[f])[:HALO]
            rows_s[c, put, :] = coded(field_part(last, slots, f, sixteen, lanes), SCALES[f])[16 - HALO:]
        for ref, out in ((rows_n, north_out), (rows_s, south_out)):
            ref[c, rest, :] = jnp.zeros((ROW_BLOCK - ROW_FIELDS * HALO, LANES), jnp.int32)
            out[pl.ds(0, ROW_BLOCK), lanes] = ref[c].astype(jnp.int16)
            out[pl.ds(ROW_BLOCK, 16), lanes] = jnp.zeros((16, LANES), jnp.int16)


def decode(value, f):
    return value.astype(jnp.float32) * (1.0 / SCALES[f])


def same(value, *_):
    return value


BODY = pl.ds(HALO, CY)
TOP = pl.ds(0, HALO)
BOTTOM = pl.ds(HALO + CY, HALO)


def column_halo(nat, east, west, f0, f1, fill, fix=same):
    group = lane_ids(EXT) // COLS
    x = jnp.full((EXT, LANES), fill, jnp.float32)
    for f, ref, table, at in ((f1, east, FROM_EAST, 0), (f0, west, FROM_WEST, 3), (f0, east, FROM_EAST, 4), (f1, west, FROM_WEST, 7)):
        x = jnp.where(group == at, fix(decode(rolled(ref[...], (at - table[f]) * COLS), f)), x)
    nat[CHUNKS] = x


def tiles(step, per=5):
    def some(i, carry):
        for u in range(per):
            step(pl.multiple_of((i * per + u) * 8, 8))
        return carry

    lax.fori_loop(0, EXT // (8 * per), some, 0)


def ring(nat, dest, copy, fix=same):
    low = lane_ids(8) < 64

    def one(at):
        rows = pl.ds(at, 8)
        v = [nat[c, rows, :] for c in range(CHUNKS + 1)]
        if copy:
            for c in range(CHUNKS):
                dest[c, rows, :] = fix(v[c], c, rows)
        v = [rolled(t, 64) for t in v]
        for k in range(CHUNKS + 1):
            dest[CHUNKS + k, rows, :] = fix(jnp.where(low, v[k - 1], v[k]), CHUNKS + k, rows)

    tiles(one)


def prepare_kernel(anc, water, soak, terrain, land, east_in, west_in, north_in, south_in,
                   W, S, dgc, dgr, L, nat, east, west, rows_ns, G):
    f32 = jnp.float32
    slots = [anc[p] % 2 for p in range(2)]
    corners = pl.ds(ROW_BLOCK, 16)
    for ref, got, col in ((east, east_in, 0), (west, west_in, 1)):
        lanes = pl.ds(col * LANES, LANES)
        ref[BODY, :] = got[:, :].astype(jnp.int32)
        ref[TOP, :] = north_in[corners, lanes].astype(jnp.int32)[16 - HALO:]
        ref[BOTTOM, :] = south_in[corners, lanes].astype(jnp.int32)[:HALO]
    for c in range(CHUNKS):
        lanes = pl.ds(c * LANES, LANES)
        rows_ns[0, c] = north_in[pl.ds(0, ROW_BLOCK), lanes].astype(jnp.int32)
        rows_ns[1, c] = south_in[pl.ds(0, ROW_BLOCK), lanes].astype(jnp.int32)

    def tile_rows(dest, f, fix=same):
        for c in range(CHUNKS):
            lanes = pl.ds(c * LANES, LANES)
            dest[c, BODY, :] = field_part((water, soak, terrain, land), slots, f, pl.ds(0, CY), lanes)
            put = pl.ds(HALO * f, HALO)
            dest[c, TOP, :] = fix(decode(rows_ns[0, c, put, :], f))
            dest[c, BOTTOM, :] = fix(decode(rows_ns[1, c, put, :], f))

    guard = lambda v: jnp.maximum(v, 0.1)
    column_halo(nat, east, west, 0, 1, 0.0)
    tile_rows(W, 0)
    tile_rows(nat, 1)
    ring(nat, W, False)
    column_halo(nat, east, west, 2, 3, 1.0, guard)
    tile_rows(S, 2, guard)
    tile_rows(nat, 3, guard)
    ring(nat, S, False)
    column_halo(nat, east, west, 4, 4, 0.0)
    tile_rows(nat, 4)
    ring(nat, G, True)
    column_halo(nat, east, west, 5, 5, 0.0)
    tile_rows(nat, 5)
    ring(nat, L, True)
    for c in range(WIDE):
        G[c, pl.ds(EXT, 8), :] = jnp.zeros((8, LANES), f32)
    last_lane = lane_ids(8) == LANES - 1

    def ground_steps(at):
        rows = pl.ds(at, 8)
        g = [G[c, rows, :] for c in range(WIDE)]
        r = [rolled(v, -1) for v in g]
        for c in range(WIDE):
            dgc[c, rows, :] = jnp.where(last_lane, r[(c + 1) % WIDE], r[c]) - g[c]
            dgr[c, rows, :] = G[c, pl.ds(at + 1, 8), :] - g[c]

    tiles(ground_steps)


def step_kernel(anc, owner, cond, suction, manning, prior, land_in, seen_in, rain, rain_n, rain_s, W_in, S_in, dgc, dgr, L,
                depth_out, soak_out, misfit_out,
                land, seen, sems, nat, east, west, W, S, R, flux, coef):
    f32 = jnp.float32
    copies = [
        pltpu.make_async_copy(src, dst, sems.at[i])
        for i, (src, dst) in enumerate(((land_in, land), (seen_in, seen)))
    ]
    for copy in copies:
        copy.start()
    slots = [anc[p] % 2 for p in range(2)]
    lane8 = lane_ids(8)
    low = lane8 < 64
    last_lane = lane8 == LANES - 1
    first_lane = lane8 == 0

    for ref, col in ((east, 0), (west, 1)):
        for d in range(CY // SHARD):
            for half in range(2):
                lanes = pl.ds((col * 2 + half) * LANES, LANES)
                part = rain[d % 4, d // 4, pl.ds(2 * SHARD, 16), lanes]
                ref[pl.ds(HALO + SHARD * d + 16 * half, 16), :] = part.astype(jnp.int32)
        early = pl.ds(col * 2 * LANES, LANES)
        late = pl.ds((col * 2 + 1) * LANES, LANES)
        ref[TOP, :] = rain_n[pl.ds(32, 16), late].astype(jnp.int32)[16 - HALO:]
        ref[BOTTOM, :] = rain_s[pl.ds(32, 16), early].astype(jnp.int32)[:HALO]
    for h in range(HOURS):
        f = ROW_FIELDS + h
        column_halo(nat, east, west, f, f, 0.0)
        for c in range(CHUNKS):
            lanes = pl.ds(c * LANES, LANES)
            for d in range(CY // SHARD):
                part = rain[d % 4, d // 4, pl.ds(SHARD * h, SHARD), lanes]
                nat[c, pl.ds(HALO + SHARD * d, SHARD), :] = decode(part.astype(jnp.int32), f)
            nat[c, TOP, :] = decode(rain_n[pl.ds(16 * h, 16), lanes].astype(jnp.int32)[16 - HALO:], f)
            nat[c, BOTTOM, :] = decode(rain_s[pl.ds(16 * h, 16), lanes].astype(jnp.int32)[:HALO], f)
        ring(nat, R.at[h], True, lambda v, c, rows: jnp.where(L[c, rows, :] > 0.0, v * TIME_STEP, WATER_BODY))
    for c in range(WIDE):
        W[c, pl.ds(EXT, 8), :] = jnp.zeros((8, LANES), f32)
        flux[c, pl.ds(0, 8), :] = jnp.zeros((8, LANES), f32)

    def copy_in(at):
        rows = pl.ds(at, 8)
        for c in range(WIDE):
            W[c, rows, :] = W_in[c, rows, :]
            S[c, rows, :] = S_in[c, rows, :]

    tiles(copy_in)

    for k in range(3):
        pair = []
        for p in range(2):
            o = owner[slots[p]]
            if k == 0:
                pair.append(jnp.full((8, LANES), TIME_STEP * 0.5 ** (5.0 / 3.0), f32) / jnp.full((8, LANES), manning[o], f32))
            elif k == 1:
                pair.append(jnp.full((8, LANES), TIME_STEP * cond[o], f32))
            else:
                pair.append(jnp.full((8, LANES), TIME_STEP * cond[o] * suction[o], f32))
        for c in range(WIDE):
            v = pair[0] if c < CHUNKS else pair[1]
            if c == CHUNKS:
                v = jnp.where(lane8 < 32, pair[0], pair[1])
            if c == WIDE - 1:
                v = jnp.where(lane8 < 96, pair[1], pair[0])
            coef[k, c] = v

    def face(a, b, dg):
        total = a + b
        slope = (b - a) + dg
        return jnp.exp2(lax.log2(total) * (5.0 / 3.0)) * slope * lax.rsqrt(jnp.abs(slope) + SLOPE_FLOOR)

    def substep(h):
        def one(at):
            rows = pl.ds(at, 8)
            w = [W[c, rows, :] for c in range(WIDE)]
            r = [rolled(v, -1) for v in w]
            fe = [face(w[c], jnp.where(last_lane, r[(c + 1) % WIDE], r[c]), dgc[c, rows, :]) for c in range(WIDE)]
            r = [rolled(v, 1) for v in fe]
            for c in range(WIDE):
                fw = jnp.where(first_lane, r[c - 1], r[c])
                fs = face(w[c], W[c, pl.ds(at + 1, 8), :], dgr[c, rows, :])
                flux[c, pl.ds(at + 8, 8), :] = fs
                gain = (fe[c] - fw) + (fs - flux[c, pl.ds(at + 7, 8), :])
                ponded = jnp.maximum(w[c] + coef[0, c] * gain + R[h, c, rows, :], 0.0)
                s = S[c, rows, :]
                intake = jnp.minimum(coef[1, c] + coef[2, c] / s, ponded)
                W[c, rows, :] = ponded - intake
                S[c, rows, :] = s + intake

        tiles(one, TILES)

    def slot_one(ref, rows):
        v = [rolled(ref[CHUNKS + k, rows, :], 64) for k in range(CHUNKS + 1)]
        return [jnp.where(low, v[k], v[k + 1]) for k in range(CHUNKS)]

    def hour(h, total):
        lax.fori_loop(0, SUB, lambda i, carry: (substep(h), carry)[1], 0)

        def score(i, total):
            total = list(total)
            for half in range(2):
                start = pl.multiple_of(i * 16, 16)
                rows = pl.ds(start + half * 8, 8)
                inner = pl.ds(start + half * 8 + HALO, 8)
                ones = slot_one(W, inner)
                for c in range(CHUNKS):
                    lanes = pl.ds(c * LANES, LANES)
                    o = seen[h, 0, pl.ds(start, 16), lanes].astype(f32)[half * 8:half * 8 + 8]
                    keep = land[0, rows, lanes].astype(f32)
                    total[2] = total[2] + keep
                    for p, v in enumerate((W[c, inner, :], ones[c])):
                        depth_out[p, 0, rows, lanes] = v
                        gap = v - o
                        square = gap * gap
                        total[p] = total[p] + keep * square / (1.0 + square)
            return tuple(total)

        return lax.fori_loop(0, CY // 16, score, total)

    for copy in copies:
        copy.wait()
    zero = jnp.zeros((8, LANES), f32)
    one, two, cells = lax.fori_loop(0, HOURS, hour, (zero, zero, zero))

    def wet(i, carry):
        for u in range(4):
            start = pl.multiple_of((i * 4 + u) * 8, 8)
            rows = pl.ds(start, 8)
            inner = pl.ds(start + HALO, 8)
            ones = slot_one(S, inner)
            for c in range(CHUNKS):
                lanes = pl.ds(c * LANES, LANES)
                soak_out[0, 0, rows, lanes] = S[c, inner, :]
                soak_out[1, 0, rows, lanes] = ones[c]
        return carry

    lax.fori_loop(0, CY // 32, wet, 0)
    line = lane_ids(1)
    misfit_out[...] = jnp.where(
        line == 0,
        jnp.sum(one),
        jnp.where(line == 1, jnp.sum(two), jnp.where(line == 2, jnp.sum(cells), (prior[0] + prior[1]) * 0.5)),
    )


VM = pl.BlockSpec(memory_space=pltpu.VMEM)
SM = pl.BlockSpec(memory_space=pltpu.SMEM)


def ends(shape, where):
    pair = pl.BlockSpec((2, 1) + shape, lambda i: (0, 0) + where)
    one = pl.BlockSpec((1,) + shape, lambda i: (0,) + where)
    return [pair, pair, one, one]


def whole(shape):
    return pl.BlockSpec(shape, lambda i: (0,) * len(shape))


def pack_columns(anc, fields, forcing):
    shapes = [(CY, LANES), (CY, LANES), (HOURS, SHARD, CX)]
    return pl.pallas_call(
        columns_kernel,
        out_shape=[jax.ShapeDtypeStruct(shape, jnp.int16) for shape in shapes],
        grid=(1,),
        in_specs=[SM] + ends((CY, LANES), (0, 0)) + ends((CY, LANES), (0, CHUNKS - 1)) + [whole(forcing.shape)],
        out_specs=[whole(shape) for shape in shapes],
        name="pack_columns",
    )(anc, *fields, *fields, forcing)


def pack_rows(anc, fields):
    shape = (ROW_BLOCK + 16, CX)
    return pl.pallas_call(
        rows_kernel,
        out_shape=[jax.ShapeDtypeStruct(shape, jnp.int16)] * 2,
        grid=(1,),
        in_specs=[SM] + ends((16, CX), (0, 0)) + ends((16, CX), (CY // 16 - 1, 0)),
        out_specs=[whole(shape)] * 2,
        scratch_shapes=[pltpu.VMEM((CHUNKS, ROW_BLOCK, LANES), jnp.int32)] * 2,
        name="pack_rows",
    )(anc, *fields, *fields)


def prepare(*args):
    wide = (WIDE, EXT, LANES)
    return pl.pallas_call(
        prepare_kernel,
        out_shape=[jax.ShapeDtypeStruct(wide, jnp.float32)] * 5,
        in_specs=[SM] + [VM] * 8,
        out_specs=[VM] * 5,
        scratch_shapes=[
            pltpu.VMEM((CHUNKS + 1, EXT, LANES), jnp.float32),
            pltpu.VMEM((EXT, LANES), jnp.int32),
            pltpu.VMEM((EXT, LANES), jnp.int32),
            pltpu.VMEM((2, CHUNKS, ROW_BLOCK, LANES), jnp.int32),
            pltpu.VMEM((WIDE, EXT + 8, LANES), jnp.float32),
        ],
        compiler_params=pltpu.CompilerParams(vmem_limit_bytes=20 << 20),
        name="prepare",
    )(*args)


def steps(*args):
    f32 = jnp.float32
    tall = pltpu.VMEM((WIDE, EXT + 8, LANES), f32)
    land, seen = args[6:8]
    return pl.pallas_call(
        step_kernel,
        out_shape=(
            jax.ShapeDtypeStruct((2, 1, CY, CX), f32),
            jax.ShapeDtypeStruct((2, 1, CY, CX), f32),
            jax.ShapeDtypeStruct((1, LANES), f32),
        ),
        in_specs=[SM] * 6 + [pl.BlockSpec(memory_space=pltpu.HBM)] * 2 + [VM] * 8,
        out_specs=(VM,) * 3,
        scratch_shapes=[
            pltpu.VMEM(land.shape, land.dtype),
            pltpu.VMEM(seen.shape, seen.dtype),
            pltpu.SemaphoreType.DMA((2,)),
            pltpu.VMEM((CHUNKS + 1, EXT, LANES), f32),
            pltpu.VMEM((EXT, LANES), jnp.int32),
            pltpu.VMEM((EXT, LANES), jnp.int32),
            tall,
            pltpu.VMEM((WIDE, EXT, LANES), f32),
            pltpu.VMEM((HOURS, WIDE, EXT, LANES), f32),
            tall,
            pltpu.VMEM((3, WIDE, 8, LANES), f32),
        ],
        compiler_params=pltpu.CompilerParams(vmem_limit_bytes=24 << 20),
        name="steps",
    )(*args)


def weigh_kernel(group, lines, out):
    groups = lines.shape[1]
    table = lines[0]
    for i in range(1, lines.shape[0]):
        table = table + lines[i]
    lane = lane_ids(groups)
    pick = lambda values, at: jnp.sum(jnp.where(lane == at, values, 0.0), axis=1, keepdims=True)
    mean = 0.5 * pick(lines[0], 3)
    raw = mean * jnp.exp(-SHARPNESS * table / pick(table, 2))
    raw = jnp.where(lane < 2, raw, 0.0)
    weights = raw / jnp.sum(raw)
    mine = lax.broadcasted_iota(jnp.int32, (groups, LANES), 0) == group[0]
    for p in range(2):
        out[p] = jnp.sum(jnp.where(mine & (lane == p), weights, 0.0))


def weigh(group, lines):
    return pl.pallas_call(
        weigh_kernel,
        out_shape=jax.ShapeDtypeStruct((2,), jnp.float32),
        in_specs=[SM, VM],
        out_specs=SM,
        name="weigh",
    )(group, lines)


def route(down, right):
    pairs = []
    rows = lax.axis_size("space") // TX
    for r in range(rows):
        for c in range(TX):
            if 0 <= r + down < rows:
                pairs.append((r * TX + c, (r + down) * TX + (c + right) % TX))
    return pairs


def window(water, soak, terrain, land, forcing, seen, cond, suction, manning, owner, anc, prior):
    groups = lax.axis_size("dom")
    tiles = lax.axis_size("space")
    fields = (water, soak, terrain, land)
    to_west, to_east, rain = pack_columns(anc, fields, forcing)
    from_east = lax.ppermute(to_west, "space", route(0, -1))
    from_west = lax.ppermute(to_east, "space", route(0, 1))
    to_north, to_south = pack_rows(anc, fields)

    shard = jnp.concatenate([from_east[:16], from_east[16:32], from_west[:16], from_west[16:32]], axis=1)
    shard = jnp.concatenate([rain.reshape(HOURS * SHARD, CX), shard], axis=0)
    line = groups // 2
    partner = lax.ppermute(shard, "dom", [(i, (i + line) % groups) for i in range(groups)])

    def with_corners(block, rows):
        corner = jnp.concatenate([from_east[rows], from_west[rows]] * 2, axis=1)
        return lax.dynamic_update_slice(block, corner, (ROW_BLOCK, 0))

    from_south = lax.ppermute(with_corners(to_north, slice(0, 16)), "space", route(-1, 0))
    from_north = lax.ppermute(with_corners(to_south, slice(CY - 16, CY)), "space", route(1, 0))
    upper = lax.axis_index("dom") >= line
    pair = jnp.stack([jnp.where(upper, partner, shard), jnp.where(upper, shard, partner)])
    lines = [list(range(line)), list(range(line, groups))]
    rain = lax.all_to_all(jnp.broadcast_to(pair[None], (line,) + pair.shape), "dom", 0, 0, axis_index_groups=lines, tiled=True)

    a, b = rain[0, 0], rain[-1, -1]
    rain_south = lax.ppermute(jnp.concatenate([a[0:16], a[32:48], a[64:80]], axis=0), "space", route(-1, 0))
    rain_north = lax.ppermute(jnp.concatenate([b[16:32], b[48:64], b[64:80]], axis=0), "space", route(1, 0))
    ready = prepare(anc, *fields, from_east, from_west, from_north, from_south)
    depth, wet, score = steps(anc, owner, cond, suction, manning, prior, land, seen, rain, rain_north, rain_south, *ready)

    score = score + lax.ppermute(score, "space", [(i, i ^ 1) for i in range(tiles)])
    peers = [[t * groups + d for t in range(k, tiles, 2) for d in range(groups)] for k in range(2)]
    lines = jnp.broadcast_to(score[None], (tiles // 2 * groups, 1, LANES))
    lines = lax.all_to_all(lines, ("space", "dom"), 0, 0, axis_index_groups=peers, tiled=True)
    weights = weigh(lax.axis_index("dom")[None], lines.reshape(tiles // 2, groups, LANES))
    return depth, wet, weights


def solution(mesh):
    return jax.shard_map(
        window,
        mesh=mesh,
        in_specs=(
            P("dom", "space", None, None),
            P("dom", "space", None, None),
            P("space", None, None),
            P("space", None, None),
            P(None, None, "space", "dom", None),
            P(None, "space", None, None),
            P(),
            P(),
            P(),
            P("dom"),
            P("dom"),
            P("dom"),
        ),
        out_specs=(P("dom", "space", None, None), P("dom", "space", None, None), P("dom")),
        check_vma=False,
    )
```

```python
import jax
import jax.numpy as jnp
from jax import lax
from jax.experimental import pallas as pl
from jax.experimental.pallas import tpu as pltpu
from jax.sharding import PartitionSpec as P


TX = 4
SUB = 6
HOURS = 2
TIME_STEP = 0.01
SLOPE_FLOOR = 0.1
SHARPNESS = 20.0

CY, CX = 256, 512
HALO = SUB * HOURS
COLS = 16
EXT = CY + 2 * HALO
LANES = 128
CHUNKS = CX // LANES
TILES = 7
NARROW = 4
NARROW_TILES = 11
WIDE = 2 * CHUNKS + 1

RAIN_SCALE = 4096.0
WATER_SCALE = 20000.0
SOAK_SCALE = 16000.0
GROUND_SCALE = 10000.0

ROW_FIELDS = 6
ROW_BLOCK = 80
SHARD = 32
WATER_BODY = -1e30
SCALES = (WATER_SCALE, WATER_SCALE, SOAK_SCALE, SOAK_SCALE, GROUND_SCALE, 1.0, RAIN_SCALE, RAIN_SCALE)
FROM_EAST = (4, 0, 5, 1, 2, 6, 3, 7)
FROM_WEST = (3, 7, 2, 6, 1, 5, 0, 4)


def lane_ids(rows):
    return lax.broadcasted_iota(jnp.int32, (rows, LANES), 1)


def coded(value, scale):
    scaled = value * scale
    return (scaled + jnp.where(scaled >= 0, 0.5, -0.5)).astype(jnp.int32)


def rolled(value, shift, axis=1):
    shift = shift % value.shape[axis]
    return value if shift == 0 else pltpu.roll(value, shift, axis)


def field_part(refs, slots, field, rows, lanes):
    water, soak, terrain, land = refs
    if field < 2:
        return water[slots[field], 0, rows, lanes]
    if field < 4:
        return soak[slots[field - 2], 0, rows, lanes]
    if field == 4:
        return terrain[0, rows, lanes]
    return land[0, rows, lanes].astype(jnp.float32)


def columns_kernel(anc, *refs):
    first, last = refs[:4], refs[4:8]
    forcing, west_out, east_out, rain_out = refs[8:]
    slots = [anc[p] % 2 for p in range(2)]
    every = pl.ds(0, LANES)
    for h in range(HOURS):
        net = forcing[h, 0, 0].astype(jnp.float32) - forcing[h, 1, 0].astype(jnp.float32)
        rain_out[h] = coded(net, RAIN_SCALE).astype(jnp.int16)

    group = lane_ids(SHARD) // COLS

    def scales(table):
        line = jnp.zeros((SHARD, LANES), jnp.float32)
        for f in range(ROW_FIELDS):
            line = jnp.where(group == table[f], SCALES[f], line)
        return line

    west_scale, east_scale = scales(FROM_EAST), scales(FROM_WEST)

    def edges(d, carry):
        rows = pl.ds(pl.multiple_of(d * SHARD, SHARD), SHARD)
        to_west = jnp.zeros((SHARD, LANES), jnp.float32)
        to_east = jnp.zeros((SHARD, LANES), jnp.float32)
        for f in range(ROW_FIELDS):
            at = FROM_EAST[f]
            to_west = jnp.where(group == at, rolled(field_part(first, slots, f, rows, every), at * COLS), to_west)
            at = FROM_WEST[f]
            to_east = jnp.where(group == at, rolled(field_part(last, slots, f, rows, every), (at + 1) * COLS - LANES), to_east)
        west_out[rows, :] = coded(to_west, west_scale).astype(jnp.int16)
        east_out[rows, :] = coded(to_east, east_scale).astype(jnp.int16)
        return carry

    lax.fori_loop(0, CY // SHARD, edges, 0)

    rows = pl.ds(0, SHARD)
    to_west = west_out[rows, :].astype(jnp.int32)
    to_east = east_out[rows, :].astype(jnp.int32)
    for h in range(HOURS):
        at = FROM_EAST[ROW_FIELDS + h]
        a = rain_out[h, :, pl.ds(0, LANES)].astype(jnp.int32)
        to_west = jnp.where(group == at, rolled(a, at * COLS), to_west)
        at = FROM_WEST[ROW_FIELDS + h]
        b = rain_out[h, :, pl.ds(CX - LANES, LANES)].astype(jnp.int32)
        to_east = jnp.where(group == at, rolled(b, (at + 1) * COLS - LANES), to_east)
    west_out[rows, :] = to_west.astype(jnp.int16)
    east_out[rows, :] = to_east.astype(jnp.int16)


def rows_kernel(anc, *refs):
    first, last = refs[:4], refs[4:8]
    north_out, south_out, rows_n, rows_s = refs[8:]
    slots = [anc[p] % 2 for p in range(2)]
    rest = pl.ds(ROW_FIELDS * HALO, ROW_BLOCK - ROW_FIELDS * HALO)
    sixteen = pl.ds(0, 16)
    for c in range(CHUNKS):
        lanes = pl.ds(c * LANES, LANES)
        for f in range(ROW_FIELDS):
            put = pl.ds(HALO * f, HALO)
            rows_n[c, put, :] = coded(field_part(first, slots, f, sixteen, lanes), SCALES[f])[:HALO]
            rows_s[c, put, :] = coded(field_part(last, slots, f, sixteen, lanes), SCALES[f])[16 - HALO:]
        for ref, out in ((rows_n, north_out), (rows_s, south_out)):
            ref[c, rest, :] = jnp.zeros((ROW_BLOCK - ROW_FIELDS * HALO, LANES), jnp.int32)
            out[pl.ds(0, ROW_BLOCK), lanes] = ref[c].astype(jnp.int16)
            out[pl.ds(ROW_BLOCK, 16), lanes] = jnp.zeros((16, LANES), jnp.int16)


def decode(value, f):
    return value.astype(jnp.float32) * (1.0 / SCALES[f])


def same(value, *_):
    return value


BODY = pl.ds(HALO, CY)
TOP = pl.ds(0, HALO)
BOTTOM = pl.ds(HALO + CY, HALO)


def column_halo(nat, east, west, f0, f1, fill, fix=same):
    group = lane_ids(EXT) // COLS
    x = jnp.full((EXT, LANES), fill, jnp.float32)
    for f, ref, table, at in ((f1, east, FROM_EAST, 0), (f0, west, FROM_WEST, 3), (f0, east, FROM_EAST, 4), (f1, west, FROM_WEST, 7)):
        x = jnp.where(group == at, fix(decode(rolled(ref[...], (at - table[f]) * COLS), f)), x)
    nat[CHUNKS] = x


def tiles(step, per=5, skip=0):
    def some(i, carry):
        for u in range(per):
            step(pl.multiple_of((i * per + u) * 8 + skip, 8))
        return carry

    lax.fori_loop(0, (EXT - 2 * skip) // (8 * per), some, 0)


def slot_one(ref, rows):
    low = lane_ids(8) < 64
    v = [rolled(ref[CHUNKS + k, rows, :], 64) for k in range(CHUNKS + 1)]
    return [jnp.where(low, v[k], v[k + 1]) for k in range(CHUNKS)]


def ring(nat, dest, copy, fix=same):
    low = lane_ids(8) < 64

    def one(at):
        rows = pl.ds(at, 8)
        v = [nat[c, rows, :] for c in range(CHUNKS + 1)]
        if copy:
            for c in range(CHUNKS):
                dest[c, rows, :] = fix(v[c], c, rows)
        v = [rolled(t, 64) for t in v]
        for k in range(CHUNKS + 1):
            dest[CHUNKS + k, rows, :] = fix(jnp.where(low, v[k - 1], v[k]), CHUNKS + k, rows)

    tiles(one)


def prepare_kernel(anc, water, soak, terrain, land, east_in, west_in, north_in, south_in,
                   W, S, dgc, dgr, L, nat, east, west, rows_ns, G):
    f32 = jnp.float32
    slots = [anc[p] % 2 for p in range(2)]
    corners = pl.ds(ROW_BLOCK, 16)
    for ref, got, col in ((east, east_in, 0), (west, west_in, 1)):
        lanes = pl.ds(col * LANES, LANES)
        ref[BODY, :] = got[:, :].astype(jnp.int32)
        ref[TOP, :] = north_in[corners, lanes].astype(jnp.int32)[16 - HALO:]
        ref[BOTTOM, :] = south_in[corners, lanes].astype(jnp.int32)[:HALO]
    for c in range(CHUNKS):
        lanes = pl.ds(c * LANES, LANES)
        rows_ns[0, c] = north_in[pl.ds(0, ROW_BLOCK), lanes].astype(jnp.int32)
        rows_ns[1, c] = south_in[pl.ds(0, ROW_BLOCK), lanes].astype(jnp.int32)

    def tile_rows(dest, f, fix=same):
        for c in range(CHUNKS):
            lanes = pl.ds(c * LANES, LANES)
            dest[c, BODY, :] = field_part((water, soak, terrain, land), slots, f, pl.ds(0, CY), lanes)
            put = pl.ds(HALO * f, HALO)
            dest[c, TOP, :] = fix(decode(rows_ns[0, c, put, :], f))
            dest[c, BOTTOM, :] = fix(decode(rows_ns[1, c, put, :], f))

    guard = lambda v: jnp.maximum(v, 0.1)
    column_halo(nat, east, west, 0, 1, 0.0)
    tile_rows(W, 0)
    tile_rows(nat, 1)
    ring(nat, W, False)
    column_halo(nat, east, west, 2, 3, 1.0, guard)
    tile_rows(S, 2, guard)
    tile_rows(nat, 3, guard)
    ring(nat, S, False)
    column_halo(nat, east, west, 4, 4, 0.0)
    tile_rows(nat, 4)
    ring(nat, G, True)
    column_halo(nat, east, west, 5, 5, 0.0)
    tile_rows(nat, 5)
    ring(nat, L, True)
    for c in range(WIDE):
        G[c, pl.ds(EXT, 8), :] = jnp.zeros((8, LANES), f32)
    last_lane = lane_ids(8) == LANES - 1

    def ground_steps(at):
        rows = pl.ds(at, 8)
        g = [G[c, rows, :] for c in range(WIDE)]
        r = [rolled(v, -1) for v in g]
        for c in range(WIDE):
            dgc[c, rows, :] = jnp.where(last_lane, r[(c + 1) % WIDE], r[c]) - g[c]
            dgr[c, rows, :] = G[c, pl.ds(at + 1, 8), :] - g[c]

    tiles(ground_steps)


def step_kernel(anc, owner, cond, suction, manning, prior, land_in, seen_in, rain, rain_n, rain_s, W_in, S_in, dgc, dgr, L,
                W, S, misfit_out,
                land, seen, sems, nat, east, west, R, flux, coef):
    f32 = jnp.float32
    copies = [
        pltpu.make_async_copy(src, dst, sems.at[i])
        for i, (src, dst) in enumerate(((land_in, land), (seen_in, seen)))
    ]
    for copy in copies:
        copy.start()
    slots = [anc[p] % 2 for p in range(2)]
    lane8 = lane_ids(8)
    last_lane = lane8 == LANES - 1
    first_lane = lane8 == 0

    for ref, col in ((east, 0), (west, 1)):
        for d in range(CY // SHARD):
            for half in range(2):
                lanes = pl.ds((col * 2 + half) * LANES, LANES)
                part = rain[d % 4, d // 4, pl.ds(2 * SHARD, 16), lanes]
                ref[pl.ds(HALO + SHARD * d + 16 * half, 16), :] = part.astype(jnp.int32)
        early = pl.ds(col * 2 * LANES, LANES)
        late = pl.ds((col * 2 + 1) * LANES, LANES)
        ref[TOP, :] = rain_n[pl.ds(32, 16), late].astype(jnp.int32)[16 - HALO:]
        ref[BOTTOM, :] = rain_s[pl.ds(32, 16), early].astype(jnp.int32)[:HALO]
    for h in range(HOURS):
        f = ROW_FIELDS + h
        column_halo(nat, east, west, f, f, 0.0)
        for c in range(CHUNKS):
            lanes = pl.ds(c * LANES, LANES)
            for d in range(CY // SHARD):
                part = rain[d % 4, d // 4, pl.ds(SHARD * h, SHARD), lanes]
                nat[c, pl.ds(HALO + SHARD * d, SHARD), :] = decode(part.astype(jnp.int32), f)
            nat[c, TOP, :] = decode(rain_n[pl.ds(16 * h, 16), lanes].astype(jnp.int32)[16 - HALO:], f)
            nat[c, BOTTOM, :] = decode(rain_s[pl.ds(16 * h, 16), lanes].astype(jnp.int32)[:HALO], f)
        ring(nat, R.at[h], True, lambda v, c, rows: jnp.where(L[c, rows, :] > 0.0, v * TIME_STEP, WATER_BODY))
    for c in range(WIDE):
        W[c, pl.ds(EXT, 8), :] = jnp.zeros((8, LANES), f32)
        flux[c, pl.ds(0, 8), :] = jnp.zeros((8, LANES), f32)

    def copy_in(at):
        rows = pl.ds(at, 8)
        for c in range(WIDE):
            W[c, rows, :] = W_in[c, rows, :]
            S[c, rows, :] = S_in[c, rows, :]

    tiles(copy_in)

    for k in range(3):
        pair = []
        for p in range(2):
            o = owner[slots[p]]
            if k == 0:
                pair.append(jnp.full((8, LANES), TIME_STEP * 0.5 ** (5.0 / 3.0), f32) / jnp.full((8, LANES), manning[o], f32))
            elif k == 1:
                pair.append(jnp.full((8, LANES), TIME_STEP * cond[o], f32))
            else:
                pair.append(jnp.full((8, LANES), TIME_STEP * cond[o] * suction[o], f32))
        for c in range(WIDE):
            v = pair[0] if c < CHUNKS else pair[1]
            if c == CHUNKS:
                v = jnp.where(lane8 < 32, pair[0], pair[1])
            if c == WIDE - 1:
                v = jnp.where(lane8 < 96, pair[1], pair[0])
            coef[k, c] = v

    def face(a, b, dg):
        total = a + b
        slope = (b - a) + dg
        return jnp.exp2(lax.log2(total) * (5.0 / 3.0)) * slope * lax.rsqrt(jnp.abs(slope) + SLOPE_FLOOR)

    def substep(h, start, per):
        def one(at):
            rows = pl.ds(at, 8)
            w = [W[c, rows, :] for c in range(WIDE)]
            r = [rolled(v, -1) for v in w]
            fe = [face(w[c], jnp.where(last_lane, r[(c + 1) % WIDE], r[c]), dgc[c, rows, :]) for c in range(WIDE)]
            r = [rolled(v, 1) for v in fe]
            for c in range(WIDE):
                fw = jnp.where(first_lane, r[c - 1], r[c])
                fs = face(w[c], W[c, pl.ds(at + 1, 8), :], dgr[c, rows, :])
                flux[c, pl.ds(at + 8, 8), :] = fs
                gain = (fe[c] - fw) + (fs - flux[c, pl.ds(at + 7, 8), :])
                ponded = jnp.maximum(w[c] + coef[0, c] * gain + R[h, c, rows, :], 0.0)
                s = S[c, rows, :]
                intake = jnp.minimum(coef[1, c] + coef[2, c] / s, ponded)
                W[c, rows, :] = ponded - intake
                S[c, rows, :] = s + intake

        tiles(one, per, start)

    def score(h, total):
        def some(i, total):
            total = list(total)
            for part in range(4):
                start = pl.multiple_of(i * 32 + part // 2 * 16, 16)
                rows = pl.ds(start + part % 2 * 8, 8)
                inner = pl.ds(start + part % 2 * 8 + HALO, 8)
                ones = slot_one(W, inner)
                for c in range(CHUNKS):
                    lanes = pl.ds(c * LANES, LANES)
                    o = seen[h, 0, pl.ds(start, 16), lanes].astype(f32)[part % 2 * 8:part % 2 * 8 + 8]
                    keep = land[0, rows, lanes].astype(f32)
                    total[2] = total[2] + keep
                    for p, v in enumerate((W[c, inner, :], ones[c])):
                        gap = v - o
                        square = gap * gap
                        total[p] = total[p] + keep * square / (1.0 + square)
            return tuple(total)

        return lax.fori_loop(0, CY // 32, some, total)

    def repeat(times, step):
        lax.fori_loop(0, times, lambda i, carry: (step(), carry)[1], 0)

    for copy in copies:
        copy.wait()
    zero = jnp.zeros((8, LANES), f32)

    def hour(h, total):
        repeat(SUB - NARROW, lambda: substep(h, 0, TILES))
        lax.cond(
            h == HOURS - 1,
            lambda: repeat(NARROW, lambda: substep(h, 8, NARROW_TILES)),
            lambda: repeat(NARROW, lambda: substep(h, 0, TILES)),
        )
        return score(h, total)

    one, two, cells = lax.fori_loop(0, HOURS, hour, (zero, zero, zero))
    line = lane_ids(1)
    misfit_out[...] = jnp.where(
        line == 0,
        jnp.sum(one),
        jnp.where(line == 1, jnp.sum(two), jnp.where(line == 2, jnp.sum(cells), (prior[0] + prior[1]) * 0.5)),
    )


def finish_kernel(W, S, depth_out, soak_out):
    def some(i, carry):
        for u in range(4):
            start = pl.multiple_of((i * 4 + u) * 8, 8)
            rows = pl.ds(start, 8)
            inner = pl.ds(start + HALO, 8)
            for ref, out in ((W, depth_out), (S, soak_out)):
                ones = slot_one(ref, inner)
                for c in range(CHUNKS):
                    lanes = pl.ds(c * LANES, LANES)
                    out[0, 0, rows, lanes] = ref[c, inner, :]
                    out[1, 0, rows, lanes] = ones[c]
        return carry

    lax.fori_loop(0, CY // 32, some, 0)


VM = pl.BlockSpec(memory_space=pltpu.VMEM)
SM = pl.BlockSpec(memory_space=pltpu.SMEM)


def ends(shape, where):
    pair = pl.BlockSpec((2, 1) + shape, lambda i: (0, 0) + where)
    one = pl.BlockSpec((1,) + shape, lambda i: (0,) + where)
    return [pair, pair, one, one]


def whole(shape):
    return pl.BlockSpec(shape, lambda i: (0,) * len(shape))


def pack_columns(anc, fields, forcing):
    shapes = [(CY, LANES), (CY, LANES), (HOURS, SHARD, CX)]
    return pl.pallas_call(
        columns_kernel,
        out_shape=[jax.ShapeDtypeStruct(shape, jnp.int16) for shape in shapes],
        grid=(1,),
        in_specs=[SM] + ends((CY, LANES), (0, 0)) + ends((CY, LANES), (0, CHUNKS - 1)) + [whole(forcing.shape)],
        out_specs=[whole(shape) for shape in shapes],
        name="pack_columns",
    )(anc, *fields, *fields, forcing)


def pack_rows(anc, fields):
    shape = (ROW_BLOCK + 16, CX)
    return pl.pallas_call(
        rows_kernel,
        out_shape=[jax.ShapeDtypeStruct(shape, jnp.int16)] * 2,
        grid=(1,),
        in_specs=[SM] + ends((16, CX), (0, 0)) + ends((16, CX), (CY // 16 - 1, 0)),
        out_specs=[whole(shape)] * 2,
        scratch_shapes=[pltpu.VMEM((CHUNKS, ROW_BLOCK, LANES), jnp.int32)] * 2,
        name="pack_rows",
    )(anc, *fields, *fields)


def prepare(*args):
    wide = (WIDE, EXT, LANES)
    return pl.pallas_call(
        prepare_kernel,
        out_shape=[jax.ShapeDtypeStruct(wide, jnp.float32)] * 5,
        in_specs=[SM] + [VM] * 8,
        out_specs=[VM] * 5,
        scratch_shapes=[
            pltpu.VMEM((CHUNKS + 1, EXT, LANES), jnp.float32),
            pltpu.VMEM((EXT, LANES), jnp.int32),
            pltpu.VMEM((EXT, LANES), jnp.int32),
            pltpu.VMEM((2, CHUNKS, ROW_BLOCK, LANES), jnp.int32),
            pltpu.VMEM((WIDE, EXT + 8, LANES), jnp.float32),
        ],
        compiler_params=pltpu.CompilerParams(vmem_limit_bytes=20 << 20),
        name="prepare",
    )(*args)


def steps(*args):
    f32 = jnp.float32
    land, seen = args[6:8]
    return pl.pallas_call(
        step_kernel,
        out_shape=(
            jax.ShapeDtypeStruct((WIDE, EXT + 8, LANES), f32),
            jax.ShapeDtypeStruct((WIDE, EXT, LANES), f32),
            jax.ShapeDtypeStruct((1, LANES), f32),
        ),
        in_specs=[SM] * 6 + [pl.BlockSpec(memory_space=pltpu.HBM)] * 2 + [VM] * 8,
        out_specs=(VM,) * 3,
        scratch_shapes=[
            pltpu.VMEM(land.shape, land.dtype),
            pltpu.VMEM(seen.shape, seen.dtype),
            pltpu.SemaphoreType.DMA((2,)),
            pltpu.VMEM((CHUNKS + 1, EXT, LANES), f32),
            pltpu.VMEM((EXT, LANES), jnp.int32),
            pltpu.VMEM((EXT, LANES), jnp.int32),
            pltpu.VMEM((HOURS, WIDE, EXT, LANES), f32),
            pltpu.VMEM((WIDE, EXT + 8, LANES), f32),
            pltpu.VMEM((3, WIDE, 8, LANES), f32),
        ],
        compiler_params=pltpu.CompilerParams(vmem_limit_bytes=14 << 20),
        name="steps",
    )(*args)


def finish(*state):
    shape = jax.ShapeDtypeStruct((2, 1, CY, CX), jnp.float32)
    return pl.pallas_call(
        finish_kernel,
        out_shape=(shape, shape),
        in_specs=[VM] * 2,
        out_specs=(VM,) * 2,
        compiler_params=pltpu.CompilerParams(vmem_limit_bytes=8 << 20),
        name="finish",
    )(*state)


def weigh_kernel(group, lines, out):
    groups = lines.shape[1]
    table = lines[0]
    for i in range(1, lines.shape[0]):
        table = table + lines[i]
    lane = lane_ids(groups)
    pick = lambda values, at: jnp.sum(jnp.where(lane == at, values, 0.0), axis=1, keepdims=True)
    mean = 0.5 * pick(lines[0], 3)
    raw = mean * jnp.exp(-SHARPNESS * table / pick(table, 2))
    raw = jnp.where(lane < 2, raw, 0.0)
    weights = raw / jnp.sum(raw)
    mine = lax.broadcasted_iota(jnp.int32, (groups, LANES), 0) == group[0]
    for p in range(2):
        out[p] = jnp.sum(jnp.where(mine & (lane == p), weights, 0.0))


def weigh(group, lines):
    return pl.pallas_call(
        weigh_kernel,
        out_shape=jax.ShapeDtypeStruct((2,), jnp.float32),
        in_specs=[SM, VM],
        out_specs=SM,
        name="weigh",
    )(group, lines)


def route(down, right):
    pairs = []
    rows = lax.axis_size("space") // TX
    for r in range(rows):
        for c in range(TX):
            if 0 <= r + down < rows:
                pairs.append((r * TX + c, (r + down) * TX + (c + right) % TX))
    return pairs


def window(water, soak, terrain, land, forcing, seen, cond, suction, manning, owner, anc, prior):
    groups = lax.axis_size("dom")
    tiles = lax.axis_size("space")
    fields = (water, soak, terrain, land)
    to_west, to_east, rain = pack_columns(anc, fields, forcing)
    from_east = lax.ppermute(to_west, "space", route(0, -1))
    from_west = lax.ppermute(to_east, "space", route(0, 1))
    to_north, to_south = pack_rows(anc, fields)

    shard = jnp.concatenate([from_east[:16], from_east[16:32], from_west[:16], from_west[16:32]], axis=1)
    shard = jnp.concatenate([rain.reshape(HOURS * SHARD, CX), shard], axis=0)
    line = groups // 2
    partner = lax.ppermute(shard, "dom", [(i, (i + line) % groups) for i in range(groups)])

    def with_corners(block, rows):
        corner = jnp.concatenate([from_east[rows], from_west[rows]] * 2, axis=1)
        return lax.dynamic_update_slice(block, corner, (ROW_BLOCK, 0))

    from_south = lax.ppermute(with_corners(to_north, slice(0, 16)), "space", route(-1, 0))
    from_north = lax.ppermute(with_corners(to_south, slice(CY - 16, CY)), "space", route(1, 0))
    upper = lax.axis_index("dom") >= line
    pair = jnp.stack([jnp.where(upper, partner, shard), jnp.where(upper, shard, partner)])
    lines = [list(range(line)), list(range(line, groups))]
    rain = lax.all_to_all(jnp.broadcast_to(pair[None], (line,) + pair.shape), "dom", 0, 0, axis_index_groups=lines, tiled=True)

    a, b = rain[0, 0], rain[-1, -1]
    rain_south = lax.ppermute(jnp.concatenate([a[0:16], a[32:48], a[64:80]], axis=0), "space", route(-1, 0))
    rain_north = lax.ppermute(jnp.concatenate([b[16:32], b[48:64], b[64:80]], axis=0), "space", route(1, 0))
    ready = prepare(anc, *fields, from_east, from_west, from_north, from_south)
    *state, score = steps(anc, owner, cond, suction, manning, prior, land, seen, rain, rain_north, rain_south, *ready)

    score = score + lax.ppermute(score, "space", [(i, i ^ 1) for i in range(tiles)])
    peers = [[t * groups + d for t in range(k, tiles, 2) for d in range(groups)] for k in range(2)]
    lines = jnp.broadcast_to(score[None], (tiles // 2 * groups, 1, LANES))
    lines = lax.all_to_all(lines, ("space", "dom"), 0, 0, axis_index_groups=peers, tiled=True)
    depth, wet = finish(*state)
    weights = weigh(lax.axis_index("dom")[None], lines.reshape(tiles // 2, groups, LANES))
    return depth, wet, weights


def solution(mesh):
    return jax.shard_map(
        window,
        mesh=mesh,
        in_specs=(
            P("dom", "space", None, None),
            P("dom", "space", None, None),
            P("space", None, None),
            P("space", None, None),
            P(None, None, "space", "dom", None),
            P(None, "space", None, None),
            P(),
            P(),
            P(),
            P("dom"),
            P("dom"),
            P("dom"),
        ),
        out_specs=(P("dom", "space", None, None), P("dom", "space", None, None), P("dom")),
        check_vma=False,
    )
```

```python
import jax
import jax.numpy as jnp
from jax import lax
from jax.experimental import pallas as pl
from jax.experimental.pallas import tpu as pltpu
from jax.sharding import PartitionSpec as P


TX = 4
SUB = 6
HOURS = 2
TIME_STEP = 0.01
SLOPE_FLOOR = 0.1
SHARPNESS = 20.0

CY, CX = 256, 512
HALO = SUB * HOURS
COLS = 16
EXT = CY + 2 * HALO
LANES = 128
CHUNKS = CX // LANES
TILES = 7
NARROW = 4
NARROW_TILES = 11
WIDE = 2 * CHUNKS + 1

RAIN_SCALE = 4096.0
WATER_SCALE = 20000.0
SOAK_SCALE = 16000.0
GROUND_SCALE = 10000.0

ROW_FIELDS = 6
ROW_BLOCK = 80
SHARD = 32
WATER_BODY = -1e30
SCALES = (WATER_SCALE, WATER_SCALE, SOAK_SCALE, SOAK_SCALE, GROUND_SCALE, 1.0, RAIN_SCALE, RAIN_SCALE)
FROM_EAST = (4, 0, 5, 1, 2, 6, 3, 7)
FROM_WEST = (3, 7, 2, 6, 1, 5, 0, 4)


def lane_ids(rows):
    return lax.broadcasted_iota(jnp.int32, (rows, LANES), 1)


def coded(value, scale):
    scaled = value * scale
    return (scaled + jnp.where(scaled >= 0, 0.5, -0.5)).astype(jnp.int32)


def rolled(value, shift, axis=1):
    shift = shift % value.shape[axis]
    return value if shift == 0 else pltpu.roll(value, shift, axis)


def field_part(refs, slots, field, rows, lanes):
    water, soak, terrain, land = refs
    if field < 2:
        return water[slots[field], 0, rows, lanes]
    if field < 4:
        return soak[slots[field - 2], 0, rows, lanes]
    if field == 4:
        return terrain[0, rows, lanes]
    return land[0, rows, lanes].astype(jnp.float32)


def columns_kernel(anc, *refs):
    first, last = refs[:4], refs[4:8]
    forcing, west_out, east_out, rain_out = refs[8:]
    slots = [anc[p] % 2 for p in range(2)]
    every = pl.ds(0, LANES)
    for h in range(HOURS):
        net = forcing[h, 0, 0].astype(jnp.float32) - forcing[h, 1, 0].astype(jnp.float32)
        rain_out[h] = coded(net, RAIN_SCALE).astype(jnp.int16)

    group = lane_ids(SHARD) // COLS

    def scales(table):
        line = jnp.zeros((SHARD, LANES), jnp.float32)
        for f in range(ROW_FIELDS):
            line = jnp.where(group == table[f], SCALES[f], line)
        return line

    west_scale, east_scale = scales(FROM_EAST), scales(FROM_WEST)

    def edges(d, carry):
        rows = pl.ds(pl.multiple_of(d * SHARD, SHARD), SHARD)
        to_west = jnp.zeros((SHARD, LANES), jnp.float32)
        to_east = jnp.zeros((SHARD, LANES), jnp.float32)
        for f in range(ROW_FIELDS):
            at = FROM_EAST[f]
            to_west = jnp.where(group == at, rolled(field_part(first, slots, f, rows, every), at * COLS), to_west)
            at = FROM_WEST[f]
            to_east = jnp.where(group == at, rolled(field_part(last, slots, f, rows, every), (at + 1) * COLS - LANES), to_east)
        west_out[rows, :] = coded(to_west, west_scale).astype(jnp.int16)
        east_out[rows, :] = coded(to_east, east_scale).astype(jnp.int16)
        return carry

    lax.fori_loop(0, CY // SHARD, edges, 0)

    rows = pl.ds(0, SHARD)
    to_west = west_out[rows, :].astype(jnp.int32)
    to_east = east_out[rows, :].astype(jnp.int32)
    for h in range(HOURS):
        at = FROM_EAST[ROW_FIELDS + h]
        a = rain_out[h, :, pl.ds(0, LANES)].astype(jnp.int32)
        to_west = jnp.where(group == at, rolled(a, at * COLS), to_west)
        at = FROM_WEST[ROW_FIELDS + h]
        b = rain_out[h, :, pl.ds(CX - LANES, LANES)].astype(jnp.int32)
        to_east = jnp.where(group == at, rolled(b, (at + 1) * COLS - LANES), to_east)
    west_out[rows, :] = to_west.astype(jnp.int16)
    east_out[rows, :] = to_east.astype(jnp.int16)


def rows_kernel(anc, *refs):
    first, last = refs[:4], refs[4:8]
    north_out, south_out, rows_n, rows_s = refs[8:]
    slots = [anc[p] % 2 for p in range(2)]
    rest = pl.ds(ROW_FIELDS * HALO, ROW_BLOCK - ROW_FIELDS * HALO)
    sixteen = pl.ds(0, 16)
    for c in range(CHUNKS):
        lanes = pl.ds(c * LANES, LANES)
        for f in range(ROW_FIELDS):
            put = pl.ds(HALO * f, HALO)
            rows_n[c, put, :] = coded(field_part(first, slots, f, sixteen, lanes), SCALES[f])[:HALO]
            rows_s[c, put, :] = coded(field_part(last, slots, f, sixteen, lanes), SCALES[f])[16 - HALO:]
        for ref, out in ((rows_n, north_out), (rows_s, south_out)):
            ref[c, rest, :] = jnp.zeros((ROW_BLOCK - ROW_FIELDS * HALO, LANES), jnp.int32)
            out[pl.ds(0, ROW_BLOCK), lanes] = ref[c].astype(jnp.int16)
            out[pl.ds(ROW_BLOCK, 16), lanes] = jnp.zeros((16, LANES), jnp.int16)


def decode(value, f):
    return value.astype(jnp.float32) * (1.0 / SCALES[f])


def same(value, *_):
    return value


BODY = pl.ds(HALO, CY)
TOP = pl.ds(0, HALO)
BOTTOM = pl.ds(HALO + CY, HALO)


def column_halo(nat, east, west, f0, f1, fill, fix=same):
    group = lane_ids(EXT) // COLS
    x = jnp.full((EXT, LANES), fill, jnp.float32)
    for f, ref, table, at in ((f1, east, FROM_EAST, 0), (f0, west, FROM_WEST, 3), (f0, east, FROM_EAST, 4), (f1, west, FROM_WEST, 7)):
        x = jnp.where(group == at, fix(decode(rolled(ref[...], (at - table[f]) * COLS), f)), x)
    nat[CHUNKS] = x


def tiles(step, per=5, skip=0):
    def some(i, carry):
        for u in range(per):
            step(pl.multiple_of((i * per + u) * 8 + skip, 8))
        return carry

    lax.fori_loop(0, (EXT - 2 * skip) // (8 * per), some, 0)


def slot_one(ref, rows):
    low = lane_ids(8) < 64
    v = [rolled(ref[CHUNKS + k, rows, :], 64) for k in range(CHUNKS + 1)]
    return [jnp.where(low, v[k], v[k + 1]) for k in range(CHUNKS)]


def ring(nat, dest, copy, fix=same):
    low = lane_ids(8) < 64

    def one(at):
        rows = pl.ds(at, 8)
        v = [nat[c, rows, :] for c in range(CHUNKS + 1)]
        if copy:
            for c in range(CHUNKS):
                dest[c, rows, :] = fix(v[c], c, rows)
        v = [rolled(t, 64) for t in v]
        for k in range(CHUNKS + 1):
            dest[CHUNKS + k, rows, :] = fix(jnp.where(low, v[k - 1], v[k]), CHUNKS + k, rows)

    tiles(one)


def in_row_order(ref, out):
    def some(i, carry):
        for u in range(4):
            start = pl.multiple_of((i * 4 + u) * 8, 8)
            rows = pl.ds(start, 8)
            inner = pl.ds(start + HALO, 8)
            ones = slot_one(ref, inner)
            for c in range(CHUNKS):
                lanes = pl.ds(c * LANES, LANES)
                out[0, 0, rows, lanes] = ref[c, inner, :]
                out[1, 0, rows, lanes] = ones[c]
        return carry

    lax.fori_loop(0, CY // 32, some, 0)


def prepare_kernel(anc, water, soak, terrain, land, east_in, west_in, north_in, south_in,
                   W, S, dgc, dgr, L, nat, east, west, rows_ns, G):
    f32 = jnp.float32
    slots = [anc[p] % 2 for p in range(2)]
    corners = pl.ds(ROW_BLOCK, 16)
    for ref, got, col in ((east, east_in, 0), (west, west_in, 1)):
        lanes = pl.ds(col * LANES, LANES)
        ref[BODY, :] = got[:, :].astype(jnp.int32)
        ref[TOP, :] = north_in[corners, lanes].astype(jnp.int32)[16 - HALO:]
        ref[BOTTOM, :] = south_in[corners, lanes].astype(jnp.int32)[:HALO]
    for c in range(CHUNKS):
        lanes = pl.ds(c * LANES, LANES)
        rows_ns[0, c] = north_in[pl.ds(0, ROW_BLOCK), lanes].astype(jnp.int32)
        rows_ns[1, c] = south_in[pl.ds(0, ROW_BLOCK), lanes].astype(jnp.int32)

    def tile_rows(dest, f, fix=same):
        for c in range(CHUNKS):
            lanes = pl.ds(c * LANES, LANES)
            dest[c, BODY, :] = field_part((water, soak, terrain, land), slots, f, pl.ds(0, CY), lanes)
            put = pl.ds(HALO * f, HALO)
            dest[c, TOP, :] = fix(decode(rows_ns[0, c, put, :], f))
            dest[c, BOTTOM, :] = fix(decode(rows_ns[1, c, put, :], f))

    guard = lambda v: jnp.maximum(v, 0.1)
    column_halo(nat, east, west, 0, 1, 0.0)
    tile_rows(W, 0)
    tile_rows(nat, 1)
    ring(nat, W, False)
    column_halo(nat, east, west, 2, 3, 1.0, guard)
    tile_rows(S, 2, guard)
    tile_rows(nat, 3, guard)
    ring(nat, S, False)
    column_halo(nat, east, west, 4, 4, 0.0)
    tile_rows(nat, 4)
    ring(nat, G, True)
    column_halo(nat, east, west, 5, 5, 0.0)
    tile_rows(nat, 5)
    ring(nat, L, True)
    for c in range(WIDE):
        G[c, pl.ds(EXT, 8), :] = jnp.zeros((8, LANES), f32)
    last_lane = lane_ids(8) == LANES - 1

    def ground_steps(at):
        rows = pl.ds(at, 8)
        g = [G[c, rows, :] for c in range(WIDE)]
        r = [rolled(v, -1) for v in g]
        for c in range(WIDE):
            dgc[c, rows, :] = jnp.where(last_lane, r[(c + 1) % WIDE], r[c]) - g[c]
            dgr[c, rows, :] = G[c, pl.ds(at + 1, 8), :] - g[c]

    tiles(ground_steps)


def step_kernel(anc, owner, cond, suction, manning, prior, land_in, seen_in, rain, rain_n, rain_s, W_in, S_in, dgc, dgr, L,
                W, soak_out, misfit_out,
                land, seen, sems, nat, east, west, R, flux, coef, S):
    f32 = jnp.float32
    copies = [
        pltpu.make_async_copy(src, dst, sems.at[i])
        for i, (src, dst) in enumerate(((land_in, land), (seen_in, seen)))
    ]
    for copy in copies:
        copy.start()
    slots = [anc[p] % 2 for p in range(2)]
    lane8 = lane_ids(8)
    last_lane = lane8 == LANES - 1
    first_lane = lane8 == 0

    for ref, col in ((east, 0), (west, 1)):
        for d in range(CY // SHARD):
            for half in range(2):
                lanes = pl.ds((col * 2 + half) * LANES, LANES)
                part = rain[d % 4, d // 4, pl.ds(2 * SHARD, 16), lanes]
                ref[pl.ds(HALO + SHARD * d + 16 * half, 16), :] = part.astype(jnp.int32)
        early = pl.ds(col * 2 * LANES, LANES)
        late = pl.ds((col * 2 + 1) * LANES, LANES)
        ref[TOP, :] = rain_n[pl.ds(32, 16), late].astype(jnp.int32)[16 - HALO:]
        ref[BOTTOM, :] = rain_s[pl.ds(32, 16), early].astype(jnp.int32)[:HALO]
    for h in range(HOURS):
        f = ROW_FIELDS + h
        column_halo(nat, east, west, f, f, 0.0)
        for c in range(CHUNKS):
            lanes = pl.ds(c * LANES, LANES)
            for d in range(CY // SHARD):
                part = rain[d % 4, d // 4, pl.ds(SHARD * h, SHARD), lanes]
                nat[c, pl.ds(HALO + SHARD * d, SHARD), :] = decode(part.astype(jnp.int32), f)
            nat[c, TOP, :] = decode(rain_n[pl.ds(16 * h, 16), lanes].astype(jnp.int32)[16 - HALO:], f)
            nat[c, BOTTOM, :] = decode(rain_s[pl.ds(16 * h, 16), lanes].astype(jnp.int32)[:HALO], f)
        ring(nat, R.at[h], True, lambda v, c, rows: jnp.where(L[c, rows, :] > 0.0, v * TIME_STEP, WATER_BODY))
    for c in range(WIDE):
        W[c, pl.ds(EXT, 8), :] = jnp.zeros((8, LANES), f32)
        flux[c, pl.ds(0, 8), :] = jnp.zeros((8, LANES), f32)

    def copy_in(at):
        rows = pl.ds(at, 8)
        for c in range(WIDE):
            W[c, rows, :] = W_in[c, rows, :]
            S[c, rows, :] = S_in[c, rows, :]

    tiles(copy_in)

    for k in range(3):
        pair = []
        for p in range(2):
            o = owner[slots[p]]
            if k == 0:
                pair.append(jnp.full((8, LANES), TIME_STEP * 0.5 ** (5.0 / 3.0), f32) / jnp.full((8, LANES), manning[o], f32))
            elif k == 1:
                pair.append(jnp.full((8, LANES), TIME_STEP * cond[o], f32))
            else:
                pair.append(jnp.full((8, LANES), TIME_STEP * cond[o] * suction[o], f32))
        for c in range(WIDE):
            v = pair[0] if c < CHUNKS else pair[1]
            if c == CHUNKS:
                v = jnp.where(lane8 < 32, pair[0], pair[1])
            if c == WIDE - 1:
                v = jnp.where(lane8 < 96, pair[1], pair[0])
            coef[k, c] = v

    def face(a, b, dg):
        total = a + b
        slope = (b - a) + dg
        return jnp.exp2(lax.log2(total) * (5.0 / 3.0)) * slope * lax.rsqrt(jnp.abs(slope) + SLOPE_FLOOR)

    def substep(h, start, per):
        def one(at):
            rows = pl.ds(at, 8)
            w = [W[c, rows, :] for c in range(WIDE)]
            r = [rolled(v, -1) for v in w]
            fe = [face(w[c], jnp.where(last_lane, r[(c + 1) % WIDE], r[c]), dgc[c, rows, :]) for c in range(WIDE)]
            r = [rolled(v, 1) for v in fe]
            for c in range(WIDE):
                fw = jnp.where(first_lane, r[c - 1], r[c])
                fs = face(w[c], W[c, pl.ds(at + 1, 8), :], dgr[c, rows, :])
                flux[c, pl.ds(at + 8, 8), :] = fs
                gain = (fe[c] - fw) + (fs - flux[c, pl.ds(at + 7, 8), :])
                ponded = jnp.maximum(w[c] + coef[0, c] * gain + R[h, c, rows, :], 0.0)
                s = S[c, rows, :]
                intake = jnp.minimum(coef[1, c] + coef[2, c] / s, ponded)
                W[c, rows, :] = ponded - intake
                S[c, rows, :] = s + intake

        tiles(one, per, start)

    def score(h, total):
        def some(i, total):
            total = list(total)
            for part in range(4):
                start = pl.multiple_of(i * 32 + part // 2 * 16, 16)
                rows = pl.ds(start + part % 2 * 8, 8)
                inner = pl.ds(start + part % 2 * 8 + HALO, 8)
                ones = slot_one(W, inner)
                for c in range(CHUNKS):
                    lanes = pl.ds(c * LANES, LANES)
                    o = seen[h, 0, pl.ds(start, 16), lanes].astype(f32)[part % 2 * 8:part % 2 * 8 + 8]
                    keep = land[0, rows, lanes].astype(f32)
                    total[2] = total[2] + keep
                    for p, v in enumerate((W[c, inner, :], ones[c])):
                        gap = v - o
                        square = gap * gap
                        total[p] = total[p] + keep * square / (1.0 + square)
            return tuple(total)

        return lax.fori_loop(0, CY // 32, some, total)

    def repeat(times, step):
        lax.fori_loop(0, times, lambda i, carry: (step(), carry)[1], 0)

    for copy in copies:
        copy.wait()
    zero = jnp.zeros((8, LANES), f32)

    def hour(h, total):
        repeat(SUB - NARROW, lambda: substep(h, 0, TILES))
        lax.cond(
            h == HOURS - 1,
            lambda: repeat(NARROW, lambda: substep(h, 8, NARROW_TILES)),
            lambda: repeat(NARROW, lambda: substep(h, 0, TILES)),
        )
        return score(h, total)

    one, two, cells = lax.fori_loop(0, HOURS, hour, (zero, zero, zero))
    in_row_order(S, soak_out)
    line = lane_ids(1)
    misfit_out[...] = jnp.where(
        line == 0,
        jnp.sum(one),
        jnp.where(line == 1, jnp.sum(two), jnp.where(line == 2, jnp.sum(cells), (prior[0] + prior[1]) * 0.5)),
    )


VM = pl.BlockSpec(memory_space=pltpu.VMEM)
SM = pl.BlockSpec(memory_space=pltpu.SMEM)


def ends(shape, where):
    pair = pl.BlockSpec((2, 1) + shape, lambda i: (0, 0) + where)
    one = pl.BlockSpec((1,) + shape, lambda i: (0,) + where)
    return [pair, pair, one, one]


def whole(shape):
    return pl.BlockSpec(shape, lambda i: (0,) * len(shape))


def pack_columns(anc, fields, forcing):
    shapes = [(CY, LANES), (CY, LANES), (HOURS, SHARD, CX)]
    return pl.pallas_call(
        columns_kernel,
        out_shape=[jax.ShapeDtypeStruct(shape, jnp.int16) for shape in shapes],
        grid=(1,),
        in_specs=[SM] + ends((CY, LANES), (0, 0)) + ends((CY, LANES), (0, CHUNKS - 1)) + [whole(forcing.shape)],
        out_specs=[whole(shape) for shape in shapes],
        name="pack_columns",
    )(anc, *fields, *fields, forcing)


def pack_rows(anc, fields):
    shape = (ROW_BLOCK + 16, CX)
    return pl.pallas_call(
        rows_kernel,
        out_shape=[jax.ShapeDtypeStruct(shape, jnp.int16)] * 2,
        grid=(1,),
        in_specs=[SM] + ends((16, CX), (0, 0)) + ends((16, CX), (CY // 16 - 1, 0)),
        out_specs=[whole(shape)] * 2,
        scratch_shapes=[pltpu.VMEM((CHUNKS, ROW_BLOCK, LANES), jnp.int32)] * 2,
        name="pack_rows",
    )(anc, *fields, *fields)


def prepare(*args):
    wide = (WIDE, EXT, LANES)
    return pl.pallas_call(
        prepare_kernel,
        out_shape=[jax.ShapeDtypeStruct(wide, jnp.float32)] * 5,
        in_specs=[SM] + [VM] * 8,
        out_specs=[VM] * 5,
        scratch_shapes=[
            pltpu.VMEM((CHUNKS + 1, EXT, LANES), jnp.float32),
            pltpu.VMEM((EXT, LANES), jnp.int32),
            pltpu.VMEM((EXT, LANES), jnp.int32),
            pltpu.VMEM((2, CHUNKS, ROW_BLOCK, LANES), jnp.int32),
            pltpu.VMEM((WIDE, EXT + 8, LANES), jnp.float32),
        ],
        compiler_params=pltpu.CompilerParams(vmem_limit_bytes=20 << 20),
        name="prepare",
    )(*args)


def steps(*args):
    f32 = jnp.float32
    land, seen = args[6:8]
    return pl.pallas_call(
        step_kernel,
        out_shape=(
            jax.ShapeDtypeStruct((WIDE, EXT + 8, LANES), f32),
            jax.ShapeDtypeStruct((2, 1, CY, CX), f32),
            jax.ShapeDtypeStruct((1, LANES), f32),
        ),
        in_specs=[SM] * 6 + [pl.BlockSpec(memory_space=pltpu.HBM)] * 2 + [VM] * 8,
        out_specs=(VM,) * 3,
        scratch_shapes=[
            pltpu.VMEM(land.shape, land.dtype),
            pltpu.VMEM(seen.shape, seen.dtype),
            pltpu.SemaphoreType.DMA((2,)),
            pltpu.VMEM((CHUNKS + 1, EXT, LANES), f32),
            pltpu.VMEM((EXT, LANES), jnp.int32),
            pltpu.VMEM((EXT, LANES), jnp.int32),
            pltpu.VMEM((HOURS, WIDE, EXT, LANES), f32),
            pltpu.VMEM((WIDE, EXT + 8, LANES), f32),
            pltpu.VMEM((3, WIDE, 8, LANES), f32),
            pltpu.VMEM((WIDE, EXT, LANES), f32),
        ],
        compiler_params=pltpu.CompilerParams(vmem_limit_bytes=20 << 20),
        name="steps",
    )(*args)


def finish(state):
    shape = jax.ShapeDtypeStruct((2, 1, CY, CX), jnp.float32)
    return pl.pallas_call(
        in_row_order,
        out_shape=shape,
        in_specs=[VM],
        out_specs=VM,
        compiler_params=pltpu.CompilerParams(vmem_limit_bytes=8 << 20),
        name="finish",
    )(state)


def weigh_kernel(group, lines, out):
    groups = lines.shape[1]
    table = lines[0]
    for i in range(1, lines.shape[0]):
        table = table + lines[i]
    lane = lane_ids(groups)
    pick = lambda values, at: jnp.sum(jnp.where(lane == at, values, 0.0), axis=1, keepdims=True)
    mean = 0.5 * pick(lines[0], 3)
    raw = mean * jnp.exp(-SHARPNESS * table / pick(table, 2))
    raw = jnp.where(lane < 2, raw, 0.0)
    weights = raw / jnp.sum(raw)
    mine = lax.broadcasted_iota(jnp.int32, (groups, LANES), 0) == group[0]
    for p in range(2):
        out[p] = jnp.sum(jnp.where(mine & (lane == p), weights, 0.0))


def weigh(group, lines):
    return pl.pallas_call(
        weigh_kernel,
        out_shape=jax.ShapeDtypeStruct((2,), jnp.float32),
        in_specs=[SM, VM],
        out_specs=SM,
        name="weigh",
    )(group, lines)


def route(down, right):
    pairs = []
    rows = lax.axis_size("space") // TX
    for r in range(rows):
        for c in range(TX):
            if 0 <= r + down < rows:
                pairs.append((r * TX + c, (r + down) * TX + (c + right) % TX))
    return pairs


def window(water, soak, terrain, land, forcing, seen, cond, suction, manning, owner, anc, prior):
    groups = lax.axis_size("dom")
    tiles = lax.axis_size("space")
    fields = (water, soak, terrain, land)
    to_west, to_east, rain = pack_columns(anc, fields, forcing)
    from_east = lax.ppermute(to_west, "space", route(0, -1))
    from_west = lax.ppermute(to_east, "space", route(0, 1))
    to_north, to_south = pack_rows(anc, fields)

    shard = jnp.concatenate([from_east[:16], from_east[16:32], from_west[:16], from_west[16:32]], axis=1)
    shard = jnp.concatenate([rain.reshape(HOURS * SHARD, CX), shard], axis=0)
    line = groups // 2
    partner = lax.ppermute(shard, "dom", [(i, (i + line) % groups) for i in range(groups)])

    def with_corners(block, rows):
        corner = jnp.concatenate([from_east[rows], from_west[rows]] * 2, axis=1)
        return lax.dynamic_update_slice(block, corner, (ROW_BLOCK, 0))

    from_south = lax.ppermute(with_corners(to_north, slice(0, 16)), "space", route(-1, 0))
    from_north = lax.ppermute(with_corners(to_south, slice(CY - 16, CY)), "space", route(1, 0))
    upper = lax.axis_index("dom") >= line
    pair = jnp.stack([jnp.where(upper, partner, shard), jnp.where(upper, shard, partner)])
    lines = [list(range(line)), list(range(line, groups))]
    rain = lax.all_to_all(jnp.broadcast_to(pair[None], (line,) + pair.shape), "dom", 0, 0, axis_index_groups=lines, tiled=True)

    a, b = rain[0, 0], rain[-1, -1]
    rain_south = lax.ppermute(jnp.concatenate([a[0:16], a[32:48], a[64:80]], axis=0), "space", route(-1, 0))
    rain_north = lax.ppermute(jnp.concatenate([b[16:32], b[48:64], b[64:80]], axis=0), "space", route(1, 0))
    ready = prepare(anc, *fields, from_east, from_west, from_north, from_south)
    state, wet, score = steps(anc, owner, cond, suction, manning, prior, land, seen, rain, rain_north, rain_south, *ready)

    score = score + lax.ppermute(score, "space", [(i, i ^ 1) for i in range(tiles)])
    peers = [[t * groups + d for t in range(k, tiles, 2) for d in range(groups)] for k in range(2)]
    lines = jnp.broadcast_to(score[None], (tiles // 2 * groups, 1, LANES))
    lines = lax.all_to_all(lines, ("space", "dom"), 0, 0, axis_index_groups=peers, tiled=True)
    depth = finish(state)
    weights = weigh(lax.axis_index("dom")[None], lines.reshape(tiles // 2, groups, LANES))
    return depth, wet, weights


def solution(mesh):
    return jax.shard_map(
        window,
        mesh=mesh,
        in_specs=(
            P("dom", "space", None, None),
            P("dom", "space", None, None),
            P("space", None, None),
            P("space", None, None),
            P(None, None, "space", "dom", None),
            P(None, "space", None, None),
            P(),
            P(),
            P(),
            P("dom"),
            P("dom"),
            P("dom"),
        ),
        out_specs=(P("dom", "space", None, None), P("dom", "space", None, None), P("dom")),
        check_vma=False,
    )
```
